256 devices in a mesh: tp: 2 (over core), row: 16 (over y, x), col: 8 (over z).
Axes of the slice: x: 4, y: 4, z: 8, core: 2. Of those that a mesh axis runs over, the one named last changes fastest.
Arguments:
- acts: bfloat16 [1024, 128, 4096], P(('row', 'col'), None, 'tp'), may hold values from -6 to 6
- grads: bfloat16 [1024, 128, 4096], P(('row', 'col'), None, 'tp'), may hold values from -6 to 6
- proj_in: bfloat16 [4096, 192], P('tp'), may hold values from -0.09375 to 0.09375
- proj_out: bfloat16 [4096, 64], P('tp'), may hold values from -0.09375 to 0.09375
- curvature: float32 [12288, 12288], P('row', ('tp', 'col')), may hold values from -1 to 7, as said below
Outputs:
- trailing: float32 [12288, 12288], P('row', ('tp', 'col'))
- panel: float32 [12288, 512], P('row', 'tp')
The draws below stay inside these ranges and needn't reach their ends.
Inputs may be any that keep to these rules, and one draw needn't show every extreme that they name: curvature is symmetric.
All inputs are finite; a program needn't handle non-finite values.
Results may differ from the reference program's by a relative error of at most 0.0021.
Values may be sent and summed in bfloat16 or wider, within the bound.
No kernel may reach another device: no remote copies, remote signals or barrier semaphores. Data moves between devices by JAX's collectives and lax.ppermute only.
A program may use at most 64 MiB of HBM per device.

```python
import jax
import jax.numpy as jnp
from jax import lax

D = 4096
KA = 192
KG = 64
PANEL = 512
SEQ = 128
ORDER = 12288
EXAMPLES = 1024


def draw_curvature(key, part):
    base = jax.random.fold_in(key, 31)
    noise_key, diag_key = jax.random.split(base)
    index = jnp.arange(ORDER, dtype=jnp.float32)
    distance = jnp.abs(index[:, None] - index[None, :])
    noise = jax.random.truncated_normal(noise_key, -4.0, 4.0, (ORDER, ORDER), jnp.float32)
    levels = jax.random.uniform(diag_key, (ORDER,), jnp.float32)
    reach = 64.0
    spread = (0.5 / ORDER) ** 0.5
    symmetric = (noise + noise.T) * spread
    coupled = 5.0 * jnp.exp(-distance / reach)
    return symmetric + coupled + jnp.diag(0.5 + levels)


def block_levels(rng, dims, shards, low, top_value):
    level, own = 1.0, jax.random.fold_in(rng, 6)
    for position, shards_of in shards:
        draws = jnp.exp(jax.random.uniform(jax.random.fold_in(own, position), (shards_of,), jnp.float32, low / len(shards), top_value / len(shards)))
        level = level * jnp.repeat(draws, dims[position] // shards_of).reshape([-1 if axis == position else 1 for axis in range(len(dims))])
    return level


def normal_values(key, shape, deviation, most, cuts=(), held_as=jnp.bfloat16):
    result = deviation * jax.random.normal(key, shape, jnp.float32)
    if cuts:
        result = result * block_levels(key, shape, cuts, -0.22, 0.18)
    return jnp.clip(result, -most, most).astype(held_as)


def setup_inputs(seed: int = 0) -> dict:
    key_of = jax.random.split(jax.random.key(seed), 6)
    acts = normal_values(key_of[0], (EXAMPLES, SEQ, D), 1.0, 6.0, ((0, 128), (2, 2)))
    grads = normal_values(key_of[1], (EXAMPLES, SEQ, D), 1.0, 6.0, ((0, 128), (2, 2)))
    proj_in = normal_values(key_of[2], (D, KA), D ** -0.5, 0.09375, ((0, 2),))
    proj_out = normal_values(key_of[3], (D, KG), D ** -0.5, 0.09375, ((0, 2),))
    curvature = draw_curvature(jax.random.fold_in(key_of[5], 71), 0)
    return dict(acts=acts, grads=grads, proj_in=proj_in, proj_out=proj_out, curvature=curvature)


def reference(acts, grads, proj_in, proj_out, curvature):
    examples, seq_len, width = acts.shape
    scale = (seq_len * examples) ** (-0.5)
    proj_acts = jnp.dot(acts.reshape(-1, width).astype(jnp.float32), proj_in.astype(jnp.float32), preferred_element_type=jnp.float32).reshape(examples, seq_len, -1)
    proj_grads = jnp.dot(grads.reshape(-1, width).astype(jnp.float32), proj_out.astype(jnp.float32), preferred_element_type=jnp.float32).reshape(examples, seq_len, -1)
    outer = jnp.einsum('nsi,nsj->nij', proj_acts, proj_grads, precision=lax.Precision.HIGHEST) * scale
    features = outer.reshape(examples, -1).astype(jnp.bfloat16)
    updated = curvature + jnp.dot(features.T.astype(jnp.float32), features.astype(jnp.float32), preferred_element_type=jnp.float32)
    diag_factor = jnp.linalg.cholesky(updated[:PANEL, :PANEL])
    panel = jax.scipy.linalg.solve_triangular(diag_factor, updated[:, :PANEL].T, lower=True).T
    trailing = updated - jnp.dot(panel.astype(jnp.float32), panel.T.astype(jnp.float32), precision=lax.Precision.HIGHEST, preferred_element_type=jnp.float32)
    return (trailing, panel)
```

```python
import jax
import jax.numpy as jnp
from jax import lax
from jax.experimental import pallas as pl
from jax.experimental.pallas import tpu as pltpu
from jax.sharding import PartitionSpec as P

PANEL = 512
NB = 128
PW = 16
f32 = jnp.float32
bf16 = jnp.bfloat16
HIGHEST = lax.Precision.HIGHEST
HIGH = lax.Precision.HIGH


def halves(x):
    hi = x.astype(bf16)
    return hi, (x - hi.astype(f32)).astype(bf16)


def dot3(a, b, dims):
    ah, al = halves(a)
    bh, bl = halves(b)

    def d(x, y):
        return lax.dot_general(x, y, (dims, ((), ())), preferred_element_type=f32)

    return d(ah, bh) + (d(ah, bl) + d(al, bh))


def factor_rows(rows, j):
    sub = lax.broadcasted_iota(jnp.int32, (PW, NB), 0)
    cols = [jnp.broadcast_to(rows[:, j + k : j + k + 1], (PW, NB)) for k in range(PW)]
    pivots = jnp.ones((PW, NB), f32)
    left, right = rows[:, :NB], rows[:, NB:]
    for k in range(PW):
        p = jnp.broadcast_to(cols[k][k : k + 1, :], (PW, NB))
        pivots = jnp.where(sub == k, p, pivots)
        if k == PW - 1:
            break
        m = jnp.where(sub > k, cols[k] * (1.0 / p), 0.0)
        left = left - m * left[k : k + 1, :]
        right = right - m * right[k : k + 1, :]
        for q in range(k + 1, PW):
            cols[q] = cols[q] - m * cols[q][k : k + 1, :]
    s = lax.rsqrt(pivots)
    return jnp.concatenate([left * s, right * s], axis=1)


def factor_block(x_ref):
    for j in range(0, NB, PW):
        rows = factor_rows(x_ref[j : j + PW, :], j)
        x_ref[j : j + PW, :] = rows
        if j + PW < NB:
            mh, ml = halves(rows[:, :NB])
            rh, rl = halves(rows)
            lhs = jnp.concatenate([mh, mh, ml], axis=0)
            rhs = jnp.concatenate([rh, rl, rh], axis=0)
            upd = lax.dot_general(
                lhs, rhs, (((0,), (0,)), ((), ())), preferred_element_type=f32
            )
            x_ref[j + PW :, :] = x_ref[j + PW :, :] - upd[j + PW :, :]


def factor_kernel(a_ref, o_ref, s_ref, x_ref):
    n = PANEL
    eye = (
        lax.broadcasted_iota(jnp.int32, (n, n), 0)
        == lax.broadcasted_iota(jnp.int32, (n, n), 1)
    ).astype(f32)
    s_ref[:, :n] = a_ref[...]
    s_ref[:, n:] = eye
    for o in range(0, n, NB):
        end = o + NB
        x_ref[:, :NB] = s_ref[o:end, o:end]
        x_ref[:, NB:] = eye[:NB, :NB]
        factor_block(x_ref)
        w = dot3(x_ref[:, NB:], s_ref[o:end, o : n + end], ((1,), (0,)))
        o_ref[o:end, :end] = w[:, n - o :]
        if end < n:
            o_ref[o:end, end:] = jnp.zeros((NB, n - end), f32)
            s_ref[end:, end : n + end] = s_ref[end:, end : n + end] - dot3(
                w[:, NB : n - o], w[:, NB:], ((0,), (0,))
            )


def inverse_factor(a):
    return pl.pallas_call(
        factor_kernel,
        out_shape=jax.ShapeDtypeStruct((PANEL, PANEL), f32),
        in_specs=[pl.BlockSpec(memory_space=pltpu.VMEM)],
        out_specs=pl.BlockSpec(memory_space=pltpu.VMEM),
        scratch_shapes=[
            pltpu.VMEM((PANEL, 2 * PANEL), f32),
            pltpu.VMEM((NB, 2 * NB), f32),
        ],
        compiler_params=pltpu.CompilerParams(vmem_limit_bytes=32 << 20),
        name="inverse_factor",
    )(a)


def shifts(n, k):
    return [(i, (i + k) % n) for i in range(n)]


def gather_ring(x, axis):
    n = lax.axis_size(axis)
    me = lax.axis_index(axis)
    parts = [lax.ppermute(x, axis, shifts(n, k)) for k in range(n - 1, 0, -1)] + [x]
    both = jnp.stack(parts + parts[:-1])
    return lax.dynamic_slice_in_dim(both, n - 1 - me, n, 0)


def gather_pair(x):
    other = lax.ppermute(x, "tp", [(0, 1), (1, 0)])
    first = lax.axis_index("tp") == 0
    return jnp.concatenate(
        [jnp.where(first, x, other), jnp.where(first, other, x)], axis=0
    )


def per_device(acts, grads, proj_in, proj_out, curvature):
    tp_n, row_n, col_n = (lax.axis_size(a) for a in ("tp", "row", "col"))
    tp, row, col = (lax.axis_index(a) for a in ("tp", "row", "col"))
    ex_dev, seq_len, width = acts.shape
    rows_blk, cols_blk = curvature.shape
    act_width, grad_width = proj_in.shape[1], proj_out.shape[1]
    scale = (seq_len * ex_dev * row_n * col_n) ** (-0.5)
    blocks = tp_n * col_n
    piece = PANEL // blocks
    ex = ex_dev // tp_n

    def flat(r, b):
        return ((b // col_n) * row_n + r) * col_n + b % col_n

    turn = [(flat(r, b), flat(b, r)) for r in range(row_n) for b in range(blocks)]
    axes = ("tp", "row", "col")

    lead = curvature[:, :PANEL].T
    half = PANEL // tp_n
    sent = lax.ppermute(lead[half:], "tp", [(0, 1)])
    mine = jnp.where(tp == 0, lead[:half], sent).reshape(col_n, piece, rows_blk)
    got = sum(lax.ppermute(mine[k], "col", [(0, k)]) for k in range(1, col_n))
    piece_row = jnp.where(col == 0, mine[0], got)
    piece_col = lax.ppermute(piece_row, axes, turn)
    lead_col = lax.all_gather(piece_col, "row", axis=0, tiled=True)
    diag_piece = jnp.where(row == 0, piece_row[:, :PANEL], 0.0)
    step = row_n // 2
    while step:
        pairs = [(i, i + step) for i in range(0, row_n, 2 * step)]
        diag_piece = diag_piece + lax.ppermute(diag_piece, "row", pairs)
        step //= 2
    packed = jnp.concatenate([piece_row, diag_piece], axis=1)
    packed = gather_ring(packed, "col").reshape(half, rows_blk + PANEL)
    packed = gather_pair(packed)
    lead_row, lead_diag = packed[:, :rows_blk], packed[:, rows_blk:]

    part = jnp.concatenate(
        [
            jnp.dot(acts.reshape(-1, width), proj_in, preferred_element_type=f32),
            jnp.dot(grads.reshape(-1, width), proj_out, preferred_element_type=f32),
        ],
        axis=1,
    ).reshape(tp_n, ex, seq_len, act_width + grad_width)
    first = tp == 0
    keep = jnp.where(first, part[0], part[1])
    give = jnp.where(first, part[1], part[0])
    proj = keep + lax.ppermute(give, "tp", [(0, 1), (1, 0)])
    feats = (
        jnp.einsum(
            "esi,esj->eij", proj[..., :act_width], proj[..., act_width:], precision=HIGHEST
        )
        * scale
    ).astype(bf16)
    feats = feats.reshape(ex, act_width * grad_width)

    by_block = feats.reshape(ex, blocks, cols_blk).transpose(1, 0, 2)
    lead_feats = jnp.broadcast_to(feats[None, :, :PANEL], (blocks, ex, PANEL))
    out = jnp.concatenate([by_block, lead_feats], axis=2)
    got = lax.all_to_all(out, ("tp", "col"), 0, 0, tiled=True).reshape(
        blocks * ex, cols_blk + PANEL
    )

    turned = lax.ppermute(got[:, :cols_blk], axes, turn)
    row_feats = gather_ring(turned, "col").reshape(-1, rows_blk)
    row_feats = gather_pair(row_feats)
    everyone = jnp.broadcast_to(got[None], (row_n,) + got.shape)
    got = lax.all_to_all(everyone, "row", 0, 0, tiled=True).reshape(-1, cols_blk + PANEL)
    col_feats, lead_feats = got[:, :cols_blk], got[:, cols_blk:]

    def gram(a, b):
        return lax.dot_general(a, b, (((0,), (0,)), ((), ())), preferred_element_type=f32)

    inv = inverse_factor(lead_diag + gram(lead_feats, lead_feats))
    panel_row = jnp.dot(inv, lead_row + gram(lead_feats, row_feats), precision=HIGHEST)
    panel_col = jnp.dot(inv, lead_col + gram(lead_feats, col_feats), precision=HIGHEST)
    trailing = (
        curvature
        + gram(row_feats, col_feats)
        - lax.dot_general(
            panel_row, panel_col, (((0,), (0,)), ((), ())), precision=HIGH
        )
    )
    panel = lax.dynamic_slice_in_dim(panel_row, tp * half, half, 0).T
    return (trailing, panel)


def solution(mesh):
    in_specs = (
        P(("row", "col"), None, "tp"),
        P(("row", "col"), None, "tp"),
        P("tp", None),
        P("tp", None),
        P("row", ("tp", "col")),
    )
    out_specs = (P("row", ("tp", "col")), P("row", "tp"))
    return jax.shard_map(
        per_device, mesh=mesh, in_specs=in_specs, out_specs=out_specs, check_vma=False
    )
```

```python
import jax
import jax.numpy as jnp
from jax import lax
from jax.experimental import pallas as pl
from jax.experimental.pallas import tpu as pltpu
from jax.sharding import PartitionSpec as P


PANEL = 512
NB = 128
PW = 16
f32 = jnp.float32
bf16 = jnp.bfloat16
HIGHEST = lax.Precision.HIGHEST
HIGH = lax.Precision.HIGH


def halves(x):
    hi = x.astype(bf16)
    return hi, (x - hi.astype(f32)).astype(bf16)


def dot3(a, b, dims):
    ah, al = halves(a)
    bh, bl = halves(b)

    def d(x, y):
        return lax.dot_general(x, y, (dims, ((), ())), preferred_element_type=f32)

    return d(ah, bh) + (d(ah, bl) + d(al, bh))


def factor_rows(rows, j):
    sub = lax.broadcasted_iota(jnp.int32, (PW, NB), 0)
    cols = [jnp.broadcast_to(rows[:, j + k : j + k + 1], (PW, NB)) for k in range(PW)]
    pivots = jnp.ones((PW, NB), f32)
    left, right = rows[:, :NB], rows[:, NB:]
    for k in range(PW):
        p = jnp.broadcast_to(cols[k][k : k + 1, :], (PW, NB))
        pivots = jnp.where(sub == k, p, pivots)
        if k == PW - 1:
            break
        m = jnp.where(sub > k, cols[k] * (1.0 / p), 0.0)
        left = left - m * left[k : k + 1, :]
        right = right - m * right[k : k + 1, :]
        for q in range(k + 1, PW):
            cols[q] = cols[q] - m * cols[q][k : k + 1, :]
    s = lax.rsqrt(pivots)
    return jnp.concatenate([left * s, right * s], axis=1)


def factor_block(x_ref):
    for j in range(0, NB, PW):
        rows = factor_rows(x_ref[j : j + PW, :], j)
        x_ref[j : j + PW, :] = rows
        if j + PW < NB:
            mh, ml = halves(rows[:, :NB])
            rh, rl = halves(rows)
            lhs = jnp.concatenate([mh, mh, ml], axis=0)
            rhs = jnp.concatenate([rh, rl, rh], axis=0)
            upd = lax.dot_general(
                lhs, rhs, (((0,), (0,)), ((), ())), preferred_element_type=f32
            )
            x_ref[j + PW :, :] = x_ref[j + PW :, :] - upd[j + PW :, :]


def factor_kernel(a_ref, o_ref, s_ref, x_ref):
    n = PANEL
    eye = (
        lax.broadcasted_iota(jnp.int32, (n, n), 0)
        == lax.broadcasted_iota(jnp.int32, (n, n), 1)
    ).astype(f32)
    s_ref[:, :n] = a_ref[...]
    s_ref[:, n:] = eye
    for o in range(0, n, NB):
        end = o + NB
        x_ref[:, :NB] = s_ref[o:end, o:end]
        x_ref[:, NB:] = eye[:NB, :NB]
        factor_block(x_ref)
        w = dot3(x_ref[:, NB:], s_ref[o:end, o : n + end], ((1,), (0,)))
        o_ref[o:end, :end] = w[:, n - o :]
        if end < n:
            o_ref[o:end, end:] = jnp.zeros((NB, n - end), f32)
            s_ref[end:, end : n + end] = s_ref[end:, end : n + end] - dot3(
                w[:, NB : n - o], w[:, NB:], ((0,), (0,))
            )


def inverse_factor(a):
    return pl.pallas_call(
        factor_kernel,
        out_shape=jax.ShapeDtypeStruct((PANEL, PANEL), f32),
        in_specs=[pl.BlockSpec(memory_space=pltpu.VMEM)],
        out_specs=pl.BlockSpec(memory_space=pltpu.VMEM),
        scratch_shapes=[
            pltpu.VMEM((PANEL, 2 * PANEL), f32),
            pltpu.VMEM((NB, 2 * NB), f32),
        ],
        compiler_params=pltpu.CompilerParams(vmem_limit_bytes=32 << 20),
        name="inverse_factor",
    )(a)


def wire_halves(x):
    hi = lax.reduce_precision(x, 8, 7)
    return hi.astype(bf16), (x - hi).astype(bf16)


def gather(x, axis):
    n = lax.axis_size(axis)
    return lax.all_to_all(jnp.broadcast_to(x[None], (n,) + x.shape), axis, 0, 0, tiled=True)


def gather_ring(x, axis):
    n = lax.axis_size(axis)
    me = lax.axis_index(axis)
    out = jnp.zeros((n,) + x.shape, x.dtype)
    out = lax.dynamic_update_index_in_dim(out, x, me, 0)
    for k in range(1, n):
        got = lax.ppermute(x, axis, [(i, (i + k) % n) for i in range(n)])
        out = lax.dynamic_update_index_in_dim(out, got, lax.rem(me + n - k, n), 0)
    return out


def gram(a, b):
    return lax.dot_general(a, b, (((0,), (0,)), ((), ())), preferred_element_type=f32)


def per_device(acts, grads, proj_in, proj_out, curvature):
    tp_n, row_n, col_n = (lax.axis_size(a) for a in ("tp", "row", "col"))
    tp = lax.axis_index("tp")
    ex_dev, seq_len, width = acts.shape
    rows_blk, cols_blk = curvature.shape
    act_width, grad_width = proj_in.shape[1], proj_out.shape[1]
    scale = (seq_len * ex_dev * row_n * col_n) ** (-0.5)
    blocks = tp_n * col_n
    piece = PANEL // row_n
    ex = ex_dev // tp_n
    axes = ("tp", "row", "col")
    swap = [(0, 1), (1, 0)]
    first = tp == 0

    def flat(r, b):
        return ((b // col_n) * row_n + r) * col_n + b % col_n

    turn = [(flat(r, b), flat(b, r)) for r in range(row_n) for b in range(blocks)]

    lead = curvature[:PANEL].reshape(row_n, piece, cols_blk)
    piece_col = lax.all_to_all(lead, "row", 0, 0, tiled=True)[0]

    part = jnp.concatenate(
        [
            jnp.dot(acts.reshape(-1, width), proj_in, preferred_element_type=f32),
            jnp.dot(grads.reshape(-1, width), proj_out, preferred_element_type=f32),
        ],
        axis=1,
    ).reshape(tp_n, ex, seq_len, act_width + grad_width)
    keep = jnp.where(first, part[0], part[1])
    give = jnp.where(first, part[1], part[0])
    proj = keep + lax.ppermute(give, "tp", swap)
    feats = (
        jnp.einsum(
            "esi,esj->eij", proj[..., :act_width], proj[..., act_width:], precision=HIGHEST
        )
        * scale
    ).astype(bf16)
    feats = feats.reshape(ex, act_width * grad_width)

    by_block = feats.reshape(ex, blocks, cols_blk).transpose(1, 0, 2)
    lead_feats = jnp.broadcast_to(feats[None, :, :PANEL], (blocks, ex, PANEL))
    out = jnp.concatenate([by_block, lead_feats], axis=2)
    got = lax.all_to_all(out, ("tp", "col"), 0, 0, tiled=True)
    got = got.reshape(blocks * ex, cols_blk + PANEL)

    block = tp * col_n + lax.axis_index("col")
    diag_piece = jnp.where(block == 0, piece_col[:, :PANEL], 0.0)
    diag_piece = diag_piece + lax.ppermute(diag_piece, "tp", [(0, 1)])
    step = col_n // 2
    while step:
        pairs = [(i, i + step) for i in range(0, col_n, 2 * step)]
        diag_piece = diag_piece + lax.ppermute(diag_piece, "col", pairs)
        step //= 2

    n_ex = got.shape[0]
    sent = jnp.concatenate([got, jnp.concatenate(wire_halves(diag_piece), axis=0)], axis=1)
    col_all = gather(sent, "row")
    diag = col_all[:, :, cols_blk + PANEL :].astype(f32)
    diag = (diag[:, :piece] + diag[:, piece:]).reshape(PANEL, PANEL)
    col_all = col_all.reshape(row_n * n_ex, -1)
    col_feats, lead_feats = col_all[:, :cols_blk], col_all[:, cols_blk : cols_blk + PANEL]

    piece_row = lax.ppermute(piece_col, axes, turn)
    turned = lax.ppermute(got[:, :cols_blk], axes, turn)
    mine = jnp.concatenate([turned, *wire_halves(piece_row)], axis=0)
    mine = gather_ring(mine, "col")
    lead_col = gather(piece_col, "row").reshape(-1, cols_blk)

    theirs = lax.ppermute(mine, "tp", swap)
    low, high = jnp.where(first, mine, theirs), jnp.where(first, theirs, mine)
    row_feats, lead_row = [], []
    for x in (low, high):
        row_feats.append(x[:, :n_ex].reshape(-1, rows_blk))
        x = x[:, n_ex:].astype(f32)
        lead_row.append((x[:, :piece] + x[:, piece:]).reshape(-1, rows_blk))
    row_feats, lead_row = jnp.concatenate(row_feats), jnp.concatenate(lead_row)

    inv = inverse_factor(diag + gram(lead_feats, lead_feats))
    panel_row = jnp.dot(inv, lead_row + gram(lead_feats, row_feats), precision=HIGH)
    panel_col = jnp.dot(inv, lead_col + gram(lead_feats, col_feats), precision=HIGH)
    trailing = (
        curvature
        + gram(row_feats, col_feats)
        - lax.dot_general(
            panel_row, panel_col, (((0,), (0,)), ((), ())), precision=HIGH
        )
    )
    half = PANEL // tp_n
    panel = lax.dynamic_slice_in_dim(panel_row, tp * half, half, 0).T
    return (trailing, panel)


def solution(mesh):
    in_specs = (
        P(("row", "col"), None, "tp"),
        P(("row", "col"), None, "tp"),
        P("tp", None),
        P("tp", None),
        P("row", ("tp", "col")),
    )
    out_specs = (P("row", ("tp", "col")), P("row", "tp"))

    return jax.shard_map(
        per_device, mesh=mesh, in_specs=in_specs, out_specs=out_specs, check_vma=False
    )
```

```python
import jax
import jax.numpy as jnp
from jax import lax
from jax.experimental import pallas as pl
from jax.experimental.pallas import tpu as pltpu
from jax.sharding import PartitionSpec as P


PANEL = 512
NB = 128
PW = 16
f32 = jnp.float32
bf16 = jnp.bfloat16
HIGHEST = lax.Precision.HIGHEST
HIGH = lax.Precision.HIGH


def halves(x):
    hi = x.astype(bf16)
    return hi, (x - hi.astype(f32)).astype(bf16)


def dot3(a, b, dims):
    ah, al = halves(a)
    bh, bl = halves(b)

    def d(x, y):
        return lax.dot_general(x, y, (dims, ((), ())), preferred_element_type=f32)

    return d(ah, bh) + (d(ah, bl) + d(al, bh))


def factor_rows(rows, j):
    sub = lax.broadcasted_iota(jnp.int32, (PW, NB), 0)
    cols = [jnp.broadcast_to(rows[:, j + k : j + k + 1], (PW, NB)) for k in range(PW)]
    pivots = jnp.ones((PW, NB), f32)
    left, right = rows[:, :NB], rows[:, NB:]
    for k in range(PW):
        p = jnp.broadcast_to(cols[k][k : k + 1, :], (PW, NB))
        pivots = jnp.where(sub == k, p, pivots)
        if k == PW - 1:
            break
        m = jnp.where(sub > k, cols[k] * (1.0 / p), 0.0)
        left = left - m * left[k : k + 1, :]
        right = right - m * right[k : k + 1, :]
        for q in range(k + 1, PW):
            cols[q] = cols[q] - m * cols[q][k : k + 1, :]
    s = lax.rsqrt(pivots)
    return jnp.concatenate([left * s, right * s], axis=1)


def factor_block(x_ref):
    for j in range(0, NB, PW):
        rows = factor_rows(x_ref[j : j + PW, :], j)
        x_ref[j : j + PW, :] = rows
        if j + PW < NB:
            mh, ml = halves(rows[:, :NB])
            rh, rl = halves(rows)
            lhs = jnp.concatenate([mh, mh, ml], axis=0)
            rhs = jnp.concatenate([rh, rl, rh], axis=0)
            upd = lax.dot_general(
                lhs, rhs, (((0,), (0,)), ((), ())), preferred_element_type=f32
            )
            x_ref[j + PW :, :] = x_ref[j + PW :, :] - upd[j + PW :, :]


def factor_kernel(a_ref, o_ref, s_ref, x_ref):
    n = PANEL
    eye = (
        lax.broadcasted_iota(jnp.int32, (n, n), 0)
        == lax.broadcasted_iota(jnp.int32, (n, n), 1)
    ).astype(f32)
    s_ref[:, :n] = a_ref[...]
    s_ref[:, n:] = eye
    lane = lax.broadcasted_iota(jnp.int32, (NB, n), 1)

    def block(b, carry):
        o = pl.multiple_of(b * NB, NB)
        x_ref[:, :NB] = s_ref[pl.ds(o, NB), pl.ds(o, NB)]
        x_ref[:, NB:] = eye[:NB, :NB]
        factor_block(x_ref)
        w = dot3(x_ref[:, NB:], s_ref[pl.ds(o, NB), :], ((1,), (0,)))
        o_ref[pl.ds(o, NB), :] = w[:, n:]

        @pl.when(b < n // NB - 1)
        def _():
            u = jnp.where(lane >= o + NB, w[:, :n], 0.0)
            s_ref[...] = s_ref[...] - dot3(u, w, ((0,), (0,)))

        return carry

    lax.fori_loop(0, n // NB, block, 0)


def inverse_factor(a):
    return pl.pallas_call(
        factor_kernel,
        out_shape=jax.ShapeDtypeStruct((PANEL, PANEL), f32),
        in_specs=[pl.BlockSpec(memory_space=pltpu.VMEM)],
        out_specs=pl.BlockSpec(memory_space=pltpu.VMEM),
        scratch_shapes=[
            pltpu.VMEM((PANEL, 2 * PANEL), f32),
            pltpu.VMEM((NB, 2 * NB), f32),
        ],
        compiler_params=pltpu.CompilerParams(vmem_limit_bytes=32 << 20),
        name="inverse_factor",
    )(a)


def wire_halves(x):
    hi = lax.reduce_precision(x, 8, 7)
    return hi.astype(bf16), (x - hi).astype(bf16)


def gather(x, axis):
    n = lax.axis_size(axis)
    return lax.all_to_all(jnp.broadcast_to(x[None], (n,) + x.shape), axis, 0, 0, tiled=True)


def gather_ring(x, axis):
    n = lax.axis_size(axis)
    me = lax.axis_index(axis)

    def shift(v, k):
        return lax.ppermute(v, axis, [(i, (i + k) % n) for i in range(n)])

    def put(out, v, k):
        return lax.dynamic_update_index_in_dim(out, v, lax.rem(me + n - k, n), 0)

    parts = {0: x}
    for k in (2, -2, 1, -1):
        parts[k] = shift(x, k)
    parts[3] = shift(parts[2], 1)
    parts[-3] = shift(parts[-2], -1)
    h = x.shape[0] // 2
    parts[4] = jnp.concatenate([shift(parts[2][:h], 2), shift(parts[-2][h:], -2)])
    out = jnp.zeros((n,) + x.shape, x.dtype)
    for k, v in parts.items():
        out = put(out, v, k)
    return out


def gram(a, b):
    return lax.dot_general(a, b, (((0,), (0,)), ((), ())), preferred_element_type=f32)


def per_device(acts, grads, proj_in, proj_out, curvature):
    tp_n, row_n, col_n = (lax.axis_size(a) for a in ("tp", "row", "col"))
    tp, col = lax.axis_index("tp"), lax.axis_index("col")
    ex_dev, seq_len, width = acts.shape
    rows_blk, cols_blk = curvature.shape
    act_width, grad_width = proj_in.shape[1], proj_out.shape[1]
    scale = (seq_len * ex_dev * row_n * col_n) ** (-0.5)
    blocks = tp_n * col_n
    piece = PANEL // row_n
    ex = ex_dev // tp_n
    axes = ("tp", "row", "col")
    swap = [(0, 1), (1, 0)]
    first = tp == 0

    def flat(r, b):
        return ((b // col_n) * row_n + r) * col_n + b % col_n

    turn = [(flat(r, b), flat(b, r)) for r in range(row_n) for b in range(blocks)]

    side = int(row_n**0.5)
    lead = curvature[:PANEL].reshape(side, side, piece, cols_blk)
    row = lax.axis_index("row")
    got = sum(lax.ppermute(lead[k], "row", [(0, side * k)]) for k in range(1, side))
    lead = jnp.where(row == 0, lead[0], got)
    got = sum(
        lax.ppermute(lead[k], "row", [(side * j, side * j + k) for j in range(side)])
        for k in range(1, side)
    )
    piece_col = jnp.where(lax.rem(row, side) == 0, lead[0], got)

    part = jnp.concatenate(
        [
            jnp.dot(acts.reshape(-1, width), proj_in, preferred_element_type=f32),
            jnp.dot(grads.reshape(-1, width), proj_out, preferred_element_type=f32),
        ],
        axis=1,
    ).reshape(tp_n, ex, seq_len, act_width + grad_width)
    keep = jnp.where(first, part[0], part[1])
    give = jnp.where(first, part[1], part[0])
    proj = keep + lax.ppermute(give, "tp", swap)
    feats = (
        jnp.einsum(
            "esi,esj->eij", proj[..., :act_width], proj[..., act_width:], precision=HIGHEST
        )
        * scale
    ).astype(bf16)
    feats = feats.reshape(ex, act_width * grad_width)

    by_block = feats.reshape(ex, blocks, cols_blk).transpose(1, 0, 2)
    lead_feats = jnp.broadcast_to(feats[None, :, :PANEL], (blocks, ex, PANEL))
    out = jnp.concatenate([by_block, lead_feats], axis=2)
    got = lax.all_to_all(out, ("tp", "col"), 0, 0, tiled=True)
    got = got.reshape(blocks * ex, cols_blk + PANEL)

    diag_piece = piece_col[:, :PANEL]
    got_diag = lax.ppermute(diag_piece, "tp", [(0, 1)])
    diag_piece = jnp.where(first, diag_piece, got_diag)
    got_diag = sum(lax.ppermute(diag_piece, "col", [(0, k)]) for k in range(1, col_n))
    diag_piece = jnp.where(col == 0, diag_piece, got_diag)

    n_ex = got.shape[0]
    sent = jnp.concatenate([got, jnp.concatenate(wire_halves(diag_piece), axis=0)], axis=1)
    col_all = gather(sent, "row")
    diag = col_all[:, :, cols_blk + PANEL :].astype(f32)
    diag = (diag[:, :piece] + diag[:, piece:]).reshape(PANEL, PANEL)
    col_all = col_all.reshape(row_n * n_ex, -1)
    col_feats, lead_feats = col_all[:, :cols_blk], col_all[:, cols_blk : cols_blk + PANEL]

    piece_row = lax.ppermute(piece_col, axes, turn)
    turned = lax.ppermute(got[:, :cols_blk], axes, turn)
    mine = jnp.concatenate([turned, *wire_halves(piece_row)], axis=0)
    mine = gather_ring(mine, "col")
    lead_col = gather(piece_col, "row").reshape(-1, cols_blk)

    theirs = lax.ppermute(mine, "tp", swap)
    low, high = jnp.where(first, mine, theirs), jnp.where(first, theirs, mine)
    row_feats, lead_row = [], []
    for x in (low, high):
        row_feats.append(x[:, :n_ex].reshape(-1, rows_blk))
        x = x[:, n_ex:].astype(f32)
        lead_row.append((x[:, :piece] + x[:, piece:]).reshape(-1, rows_blk))
    row_feats, lead_row = jnp.concatenate(row_feats), jnp.concatenate(lead_row)

    inv = inverse_factor(diag + gram(lead_feats, lead_feats))
    panel_row = jnp.dot(inv, lead_row + gram(lead_feats, row_feats), precision=HIGH)
    panel_col = jnp.dot(inv, lead_col + gram(lead_feats, col_feats), precision=HIGH)
    trailing = (
        curvature
        + gram(row_feats, col_feats)
        - lax.dot_general(
            panel_row, panel_col, (((0,), (0,)), ((), ())), precision=HIGH
        )
    )
    half = PANEL // tp_n
    panel = lax.dynamic_slice_in_dim(panel_row, tp * half, half, 0).T
    return (trailing, panel)


def solution(mesh):
    in_specs = (
        P(("row", "col"), None, "tp"),
        P(("row", "col"), None, "tp"),
        P("tp", None),
        P("tp", None),
        P("row", ("tp", "col")),
    )
    out_specs = (P("row", ("tp", "col")), P("row", "tp"))

    return jax.shard_map(
        per_device, mesh=mesh, in_specs=in_specs, out_specs=out_specs, check_vma=False
    )
```

```python
import jax
import jax.numpy as jnp
from jax import lax
from jax.experimental import pallas as pl
from jax.experimental.pallas import tpu as pltpu
from jax.sharding import PartitionSpec as P


PANEL = 512
NB = 128
PW = 16
f32 = jnp.float32
bf16 = jnp.bfloat16
HIGHEST = lax.Precision.HIGHEST
HIGH = lax.Precision.HIGH


def halves(x):
    hi = x.astype(bf16)
    return hi, (x - hi.astype(f32)).astype(bf16)


def dot3(a, b, dims):
    ah, al = halves(a)
    bh, bl = halves(b)

    def d(x, y):
        return lax.dot_general(x, y, (dims, ((), ())), preferred_element_type=f32)

    return d(ah, bh) + (d(ah, bl) + d(al, bh))


def factor_rows(rows, j):
    sub = lax.broadcasted_iota(jnp.int32, (PW, NB), 0)
    cols = [jnp.broadcast_to(rows[:, j + k : j + k + 1], (PW, NB)) for k in range(PW)]
    pivots = jnp.ones((PW, NB), f32)
    left, right = rows[:, :NB], rows[:, NB:]
    for k in range(PW):
        p = jnp.broadcast_to(cols[k][k : k + 1, :], (PW, NB))
        pivots = jnp.where(sub == k, p, pivots)
        if k == PW - 1:
            break
        m = jnp.where(sub > k, cols[k] * (1.0 / p), 0.0)
        left = left - m * left[k : k + 1, :]
        right = right - m * right[k : k + 1, :]
        for q in range(k + 1, PW):
            cols[q] = cols[q] - m * cols[q][k : k + 1, :]
    s = lax.rsqrt(pivots)
    return jnp.concatenate([left * s, right * s], axis=1)


def factor_block(x_ref):
    for j in range(0, NB, PW):
        rows = factor_rows(x_ref[j : j + PW, :], j)
        x_ref[j : j + PW, :] = rows
        if j + PW < NB:
            mh, ml = halves(rows[:, :NB])
            rh, rl = halves(rows)
            lhs = jnp.concatenate([mh, mh, ml], axis=0)
            rhs = jnp.concatenate([rh, rl, rh], axis=0)
            upd = lax.dot_general(
                lhs, rhs, (((0,), (0,)), ((), ())), preferred_element_type=f32
            )
            x_ref[j + PW :, :] = x_ref[j + PW :, :] - upd[j + PW :, :]


def factor_kernel(a_ref, o_ref, s_ref, x_ref):
    n = PANEL
    eye = (
        lax.broadcasted_iota(jnp.int32, (n, n), 0)
        == lax.broadcasted_iota(jnp.int32, (n, n), 1)
    ).astype(f32)
    s_ref[:, :n] = a_ref[...]
    s_ref[:, n:] = eye
    lane = lax.broadcasted_iota(jnp.int32, (NB, n), 1)

    def block(b, carry):
        o = pl.multiple_of(b * NB, NB)
        x_ref[:, :NB] = s_ref[pl.ds(o, NB), pl.ds(o, NB)]
        x_ref[:, NB:] = eye[:NB, :NB]
        factor_block(x_ref)
        w = dot3(x_ref[:, NB:], s_ref[pl.ds(o, NB), :], ((1,), (0,)))
        o_ref[pl.ds(o, NB), :] = w[:, n:]

        @pl.when(b < n // NB - 1)
        def _():
            u = jnp.where(lane >= o + NB, w[:, :n], 0.0)
            s_ref[...] = s_ref[...] - dot3(u, w, ((0,), (0,)))

        return carry

    lax.fori_loop(0, n // NB, block, 0)


def inverse_factor(a):
    return pl.pallas_call(
        factor_kernel,
        out_shape=jax.ShapeDtypeStruct((PANEL, PANEL), f32),
        in_specs=[pl.BlockSpec(memory_space=pltpu.VMEM)],
        out_specs=pl.BlockSpec(memory_space=pltpu.VMEM),
        scratch_shapes=[
            pltpu.VMEM((PANEL, 2 * PANEL), f32),
            pltpu.VMEM((NB, 2 * NB), f32),
        ],
        compiler_params=pltpu.CompilerParams(vmem_limit_bytes=32 << 20),
        name="inverse_factor",
    )(a)


def wire_halves(x):
    hi = lax.reduce_precision(x, 8, 7)
    return hi.astype(bf16), (x - hi).astype(bf16)


def gather(x, axis):
    n = lax.axis_size(axis)
    return lax.all_to_all(jnp.broadcast_to(x[None], (n,) + x.shape), axis, 0, 0, tiled=True)


def gather_ring(x, axis):
    n = lax.axis_size(axis)
    me = lax.axis_index(axis)

    def shift(v, k):
        return lax.ppermute(v, axis, [(i, (i + k) % n) for i in range(n)])

    def put(out, v, k):
        return lax.dynamic_update_index_in_dim(out, v, lax.rem(me + n - k, n), 0)

    parts = {0: x}
    for k in (2, -2, 1, -1):
        parts[k] = shift(x, k)
    parts[3] = shift(parts[2], 1)
    parts[-3] = shift(parts[-2], -1)
    h = x.shape[0] // 2
    parts[4] = jnp.concatenate([shift(parts[2][:h], 2), shift(parts[-2][h:], -2)])
    out = jnp.zeros((n,) + x.shape, x.dtype)
    for k, v in parts.items():
        out = put(out, v, k)
    return out


def gram(a, b):
    return lax.dot_general(a, b, (((0,), (0,)), ((), ())), preferred_element_type=f32)


def per_device(acts, grads, proj_in, proj_out, curvature):
    tp_n, row_n, col_n = (lax.axis_size(a) for a in ("tp", "row", "col"))
    tp = lax.axis_index("tp")
    ex_dev, seq_len, width = acts.shape
    rows_blk, cols_blk = curvature.shape
    act_width, grad_width = proj_in.shape[1], proj_out.shape[1]
    scale = (seq_len * ex_dev * row_n * col_n) ** (-0.5)
    blocks = tp_n * col_n
    piece = PANEL // row_n
    ex = ex_dev // tp_n
    axes = ("tp", "row", "col")
    swap = [(0, 1), (1, 0)]
    first = tp == 0

    def flat(r, b):
        return ((b // col_n) * row_n + r) * col_n + b % col_n

    turn = [(flat(r, b), flat(b, r)) for r in range(row_n) for b in range(blocks)]

    side = int(row_n**0.5)
    lead = curvature[:PANEL].reshape(side, side, piece, cols_blk)
    row = lax.axis_index("row")
    got = [lax.ppermute(lead[k], "row", [(0, side * k)]) for k in range(1, side)]
    lead = jnp.where(row == 0, lead[0], sum(got))
    got = sum(
        lax.ppermute(lead[k], "row", [(side * j, side * j + k) for j in range(side)])
        for k in range(1, side)
    )
    piece_col = jnp.where(lax.rem(row, side) == 0, lead[0], got)

    part = jnp.concatenate(
        [
            jnp.dot(acts.reshape(-1, width), proj_in, preferred_element_type=f32),
            jnp.dot(grads.reshape(-1, width), proj_out, preferred_element_type=f32),
        ],
        axis=1,
    ).reshape(tp_n, ex, seq_len, act_width + grad_width)
    keep = jnp.where(first, part[0], part[1])
    give = jnp.where(first, part[1], part[0])
    proj = keep + lax.ppermute(give, "tp", swap)
    feats = (
        jnp.einsum(
            "esi,esj->eij", proj[..., :act_width], proj[..., act_width:], precision=HIGHEST
        )
        * scale
    ).astype(bf16)
    feats = feats.reshape(ex, act_width * grad_width)

    by_block = feats.reshape(ex, blocks, cols_blk).transpose(1, 0, 2)
    lead_feats = jnp.broadcast_to(feats[None, :, :PANEL], (blocks, ex, PANEL))
    out = jnp.concatenate([by_block, lead_feats], axis=2)
    got = lax.all_to_all(out, ("tp", "col"), 0, 0, tiled=True)
    got = got.reshape(blocks * ex, cols_blk + PANEL)

    n_ex = got.shape[0]
    col_all = gather(got, "row").reshape(row_n * n_ex, -1)
    col_all, lead_piece = lax.optimization_barrier((col_all, piece_col))
    col_feats, lead_feats = col_all[:, :cols_blk], col_all[:, cols_blk:]

    piece_row = lax.ppermute(piece_col, axes, turn)
    diag = piece_row[:, :PANEL]
    got_diag = sum(
        lax.ppermute(diag, "row", [(0, side * k)]) for k in range(1, side)
    )
    diag = jnp.where(row == 0, diag, got_diag)
    got_diag = sum(
        lax.ppermute(diag, "row", [(side * j, side * j + k) for j in range(side)])
        for k in range(1, side)
    )
    diag = jnp.where(lax.rem(row, side) == 0, diag, got_diag)
    cut = rows_blk // 3
    packed = [v[:, i : i + cut] for v in wire_halves(diag) for i in range(0, PANEL, cut)]
    packed = jnp.concatenate(packed, axis=0)
    group = 16 * (-(-packed.shape[0] // 48))
    packed = jnp.pad(packed, ((0, 3 * group - packed.shape[0]), (0, 0)))
    packed = jnp.concatenate([packed[i * group : (i + 1) * group] for i in range(3)], axis=1)

    turned = lax.ppermute(got[:, :cols_blk], axes, turn)
    mine = jnp.concatenate([turned, *wire_halves(piece_row), packed], axis=0)
    mine = gather_ring(mine, "col")
    lead_col = gather(lead_piece, "row").reshape(-1, cols_blk)

    theirs = lax.ppermute(mine, "tp", swap)
    low, high = jnp.where(first, mine, theirs), jnp.where(first, theirs, mine)
    row_feats, lead_row, diag = [], [], []
    for x in (low, high):
        row_feats.append(x[:, :n_ex].reshape(-1, rows_blk))
        c = x[:, n_ex : n_ex + 2 * piece].astype(f32)
        lead_row.append((c[:, :piece] + c[:, piece:]).reshape(-1, rows_blk))
        d = x[:, n_ex + 2 * piece :]
        d = jnp.concatenate([d[:, :, i * cut : (i + 1) * cut] for i in range(3)], axis=1)
        d = d[:, : 2 * piece * PANEL // cut].astype(f32)
        d = d[:, : d.shape[1] // 2] + d[:, d.shape[1] // 2 :]
        d = jnp.concatenate([d[:, i : i + piece] for i in range(0, d.shape[1], piece)], axis=2)
        diag.append(d.reshape(-1, PANEL))
    row_feats, lead_row, diag = (jnp.concatenate(v) for v in (row_feats, lead_row, diag))

    inv = inverse_factor(diag + gram(lead_feats, lead_feats))
    panel_row = jnp.dot(inv, lead_row + gram(lead_feats, row_feats), precision=HIGH)
    panel_col = jnp.dot(inv, lead_col + gram(lead_feats, col_feats), precision=HIGH)
    trailing = (
        curvature
        + gram(row_feats, col_feats)
        - lax.dot_general(
            panel_row, panel_col, (((0,), (0,)), ((), ())), precision=HIGH
        )
    )
    half = PANEL // tp_n
    panel = lax.dynamic_slice_in_dim(panel_row, tp * half, half, 0).T
    return (trailing, panel)


def solution(mesh):
    in_specs = (
        P(("row", "col"), None, "tp"),
        P(("row", "col"), None, "tp"),
        P("tp", None),
        P("tp", None),
        P("row", ("tp", "col")),
    )
    out_specs = (P("row", ("tp", "col")), P("row", "tp"))

    return jax.shard_map(
        per_device, mesh=mesh, in_specs=in_specs, out_specs=out_specs, check_vma=False
    )
```

```python
import jax
import jax.numpy as jnp
from jax import lax
from jax.experimental import pallas as pl
from jax.experimental.pallas import tpu as pltpu
from jax.sharding import PartitionSpec as P


PANEL = 512
NB = 128
PW = 16
f32 = jnp.float32
bf16 = jnp.bfloat16
HIGHEST = lax.Precision.HIGHEST
HIGH = lax.Precision.HIGH


def halves(x):
    hi = x.astype(bf16)
    return hi, (x - hi.astype(f32)).astype(bf16)


def dot3(a, b, dims):
    ah, al = halves(a)
    bh, bl = halves(b)

    def d(x, y):
        return lax.dot_general(x, y, (dims, ((), ())), preferred_element_type=f32)

    return d(ah, bh) + (d(ah, bl) + d(al, bh))


def factor_rows(rows, j):
    sub = lax.broadcasted_iota(jnp.int32, (PW, NB), 0)
    cols = [jnp.broadcast_to(rows[:, j + k : j + k + 1], (PW, NB)) for k in range(PW)]
    pivots = jnp.ones((PW, NB), f32)
    left, right = rows[:, :NB], rows[:, NB:]
    for k in range(PW):
        p = jnp.broadcast_to(cols[k][k : k + 1, :], (PW, NB))
        pivots = jnp.where(sub == k, p, pivots)
        if k == PW - 1:
            break
        m = jnp.where(sub > k, cols[k] * (1.0 / p), 0.0)
        left = left - m * left[k : k + 1, :]
        right = right - m * right[k : k + 1, :]
        for q in range(k + 1, PW):
            cols[q] = cols[q] - m * cols[q][k : k + 1, :]
    s = lax.rsqrt(pivots)
    return jnp.concatenate([left * s, right * s], axis=1)


def factor_block(x_ref):
    for j in range(0, NB, PW):
        rows = factor_rows(x_ref[j : j + PW, :], j)
        x_ref[j : j + PW, :] = rows
        if j + PW < NB:
            mh, ml = halves(rows[:, :NB])
            rh, rl = halves(rows)
            lhs = jnp.concatenate([mh, mh, ml], axis=0)
            rhs = jnp.concatenate([rh, rl, rh], axis=0)
            upd = lax.dot_general(
                lhs, rhs, (((0,), (0,)), ((), ())), preferred_element_type=f32
            )
            x_ref[j + PW :, :] = x_ref[j + PW :, :] - upd[j + PW :, :]


def factor_kernel(a_ref, o_ref, s_ref, x_ref):
    n = PANEL
    eye = (
        lax.broadcasted_iota(jnp.int32, (n, n), 0)
        == lax.broadcasted_iota(jnp.int32, (n, n), 1)
    ).astype(f32)
    s_ref[:, :n] = a_ref[...]
    s_ref[:, n:] = eye
    lane = lax.broadcasted_iota(jnp.int32, (NB, n), 1)

    def block(b, carry):
        o = pl.multiple_of(b * NB, NB)
        x_ref[:, :NB] = s_ref[pl.ds(o, NB), pl.ds(o, NB)]
        x_ref[:, NB:] = eye[:NB, :NB]
        factor_block(x_ref)
        w = dot3(x_ref[:, NB:], s_ref[pl.ds(o, NB), :], ((1,), (0,)))
        o_ref[pl.ds(o, NB), :] = w[:, n:]

        @pl.when(b < n // NB - 1)
        def _():
            u = jnp.where(lane >= o + NB, w[:, :n], 0.0)
            s_ref[NB:, NB:] = s_ref[NB:, NB:] - dot3(u[:, NB:], w[:, NB:], ((0,), (0,)))

        return carry

    lax.fori_loop(0, n // NB, block, 0)


def inverse_factor(a):
    return pl.pallas_call(
        factor_kernel,
        out_shape=jax.ShapeDtypeStruct((PANEL, PANEL), f32),
        in_specs=[pl.BlockSpec(memory_space=pltpu.VMEM)],
        out_specs=pl.BlockSpec(memory_space=pltpu.VMEM),
        scratch_shapes=[
            pltpu.VMEM((PANEL, 2 * PANEL), f32),
            pltpu.VMEM((NB, 2 * NB), f32),
        ],
        compiler_params=pltpu.CompilerParams(vmem_limit_bytes=32 << 20),
        name="inverse_factor",
    )(a)


def wire_halves(x):
    hi = lax.reduce_precision(x, 8, 7)
    return hi.astype(bf16), (x - hi).astype(bf16)


def gather(x, axis):
    n = lax.axis_size(axis)
    return lax.all_to_all(jnp.broadcast_to(x[None], (n,) + x.shape), axis, 0, 0, tiled=True)


def gather_ring(x, axis):
    n = lax.axis_size(axis)
    me = lax.axis_index(axis)

    def shift(v, k):
        return lax.ppermute(v, axis, [(i, (i + k) % n) for i in range(n)])

    def put(out, v, k):
        return lax.dynamic_update_index_in_dim(out, v, lax.rem(me + n - k, n), 0)

    parts = {0: x}
    for k in (2, -2, 1, -1):
        parts[k] = shift(x, k)
    parts[3] = shift(parts[2], 1)
    parts[-3] = shift(parts[-2], -1)
    h = x.shape[0] // 2
    parts[4] = jnp.concatenate([shift(parts[2][:h], 2), shift(parts[-2][h:], -2)])
    out = jnp.zeros((n,) + x.shape, x.dtype)
    for k, v in parts.items():
        out = put(out, v, k)
    return out


def gram(a, b):
    return lax.dot_general(a, b, (((0,), (0,)), ((), ())), preferred_element_type=f32)


def per_device(acts, grads, proj_in, proj_out, curvature):
    tp_n, row_n, col_n = (lax.axis_size(a) for a in ("tp", "row", "col"))
    tp = lax.axis_index("tp")
    ex_dev, seq_len, width = acts.shape
    rows_blk, cols_blk = curvature.shape
    act_width, grad_width = proj_in.shape[1], proj_out.shape[1]
    scale = (seq_len * ex_dev * row_n * col_n) ** (-0.5)
    blocks = tp_n * col_n
    piece = PANEL // row_n
    ex = ex_dev // tp_n
    axes = ("tp", "row", "col")
    swap = [(0, 1), (1, 0)]
    first = tp == 0

    def flat(r, b):
        return ((b // col_n) * row_n + r) * col_n + b % col_n

    turn = [(flat(r, b), flat(b, r)) for r in range(row_n) for b in range(blocks)]

    side = int(row_n**0.5)
    lead = curvature[:PANEL].reshape(side, side, piece, cols_blk)
    row = lax.axis_index("row")
    got = [lax.ppermute(lead[k], "row", [(0, side * k)]) for k in range(1, side)]
    lead = jnp.where(row == 0, lead[0], sum(got))
    got = sum(
        lax.ppermute(lead[k], "row", [(side * j, side * j + k) for j in range(side)])
        for k in range(1, side)
    )
    piece_col = jnp.where(lax.rem(row, side) == 0, lead[0], got)

    part = jnp.concatenate(
        [
            jnp.dot(acts.reshape(-1, width), proj_in, preferred_element_type=f32),
            jnp.dot(grads.reshape(-1, width), proj_out, preferred_element_type=f32),
        ],
        axis=1,
    ).reshape(tp_n, ex, seq_len, act_width + grad_width)
    keep = jnp.where(first, part[0], part[1])
    give = jnp.where(first, part[1], part[0])
    proj = keep + lax.ppermute(give, "tp", swap)
    feats = (
        jnp.einsum(
            "esi,esj->eij", proj[..., :act_width], proj[..., act_width:], precision=HIGHEST
        )
        * scale
    ).astype(bf16)
    feats = feats.reshape(ex, act_width * grad_width)

    by_block = feats.reshape(ex, blocks, cols_blk).transpose(1, 0, 2)
    lead_feats = jnp.broadcast_to(feats[None, :, :PANEL], (blocks, ex, PANEL))
    out = jnp.concatenate([by_block, lead_feats], axis=2)
    got = lax.all_to_all(out, ("tp", "col"), 0, 0, tiled=True)
    got = got.reshape(blocks * ex, cols_blk + PANEL)

    n_ex = got.shape[0]
    col_all = gather(got, "row").reshape(row_n * n_ex, -1)
    col_all, lead_piece = lax.optimization_barrier((col_all, piece_col))
    col_feats, lead_feats = col_all[:, :cols_blk], col_all[:, cols_blk:]

    piece_row = lax.ppermute(piece_col, axes, turn)
    diag = piece_row[:, :PANEL]
    got_diag = sum(
        lax.ppermute(diag, "row", [(0, side * k)]) for k in range(1, side)
    )
    diag = jnp.where(row == 0, diag, got_diag)
    got_diag = sum(
        lax.ppermute(diag, "row", [(side * j, side * j + k) for j in range(side)])
        for k in range(1, side)
    )
    diag = jnp.where(lax.rem(row, side) == 0, diag, got_diag)
    cut = rows_blk // 3
    packed = [v[:, i : i + cut] for v in wire_halves(diag) for i in range(0, PANEL, cut)]
    packed = jnp.concatenate(packed, axis=0)
    group = 16 * (-(-packed.shape[0] // 48))
    packed = jnp.pad(packed, ((0, 3 * group - packed.shape[0]), (0, 0)))
    packed = jnp.concatenate([packed[i * group : (i + 1) * group] for i in range(3)], axis=1)

    turned = lax.ppermute(got[:, :cols_blk], axes, turn)
    mine = jnp.concatenate([turned, *wire_halves(piece_row), packed], axis=0)
    mine = gather_ring(mine, "col")
    lead_col = gather(lead_piece, "row").reshape(-1, cols_blk)

    gram_lead = gram(lead_feats, col_all)
    mine, gram_lead = lax.optimization_barrier((mine, gram_lead))
    theirs = lax.ppermute(mine, "tp", swap)
    low, high = jnp.where(first, mine, theirs), jnp.where(first, theirs, mine)
    row_feats, lead_row, diag = [], [], []
    for x in (low, high):
        row_feats.append(x[:, :n_ex].reshape(-1, rows_blk))
        c = x[:, n_ex : n_ex + 2 * piece].astype(f32)
        lead_row.append((c[:, :piece] + c[:, piece:]).reshape(-1, rows_blk))
        d = x[:, n_ex + 2 * piece :]
        d = jnp.concatenate([d[:, :, i * cut : (i + 1) * cut] for i in range(3)], axis=1)
        d = d[:, : 2 * piece * PANEL // cut].astype(f32)
        d = d[:, : d.shape[1] // 2] + d[:, d.shape[1] // 2 :]
        d = jnp.concatenate([d[:, i : i + piece] for i in range(0, d.shape[1], piece)], axis=2)
        diag.append(d.reshape(-1, PANEL))
    row_feats, lead_row, diag = (jnp.concatenate(v) for v in (row_feats, lead_row, diag))

    inv = inverse_factor(diag + gram_lead[:, cols_blk:])
    inv, lead_col = lax.optimization_barrier((inv, lead_col))
    panel_row = jnp.dot(inv, lead_row + gram(lead_feats, row_feats), precision=HIGH)
    panel_col = jnp.dot(inv, lead_col + gram_lead[:, :cols_blk], precision=HIGH)
    trailing = (
        curvature
        + gram(row_feats, col_feats)
        - lax.dot_general(
            panel_row, panel_col, (((0,), (0,)), ((), ())), precision=HIGH
        )
    )
    half = PANEL // tp_n
    panel = lax.dynamic_slice_in_dim(panel_row, tp * half, half, 0).T
    return (trailing, panel)


def solution(mesh):
    in_specs = (
        P(("row", "col"), None, "tp"),
        P(("row", "col"), None, "tp"),
        P("tp", None),
        P("tp", None),
        P("row", ("tp", "col")),
    )
    out_specs = (P("row", ("tp", "col")), P("row", "tp"))

    return jax.shard_map(
        per_device, mesh=mesh, in_specs=in_specs, out_specs=out_specs, check_vma=False
    )
```

```python
import jax
import jax.numpy as jnp
from jax import lax
from jax.experimental import pallas as pl
from jax.experimental.pallas import tpu as pltpu
from jax.sharding import PartitionSpec as P


PANEL = 512
NB = 128
PW = 16
f32 = jnp.float32
bf16 = jnp.bfloat16
HIGHEST = lax.Precision.HIGHEST
HIGH = lax.Precision.HIGH


def halves(x):
    hi = x.astype(bf16)
    return hi, (x - hi.astype(f32)).astype(bf16)


def dot3(a, b, dims):
    ah, al = halves(a)
    bh, bl = halves(b)

    def d(x, y):
        return lax.dot_general(x, y, (dims, ((), ())), preferred_element_type=f32)

    return d(ah, bh) + (d(ah, bl) + d(al, bh))


def factor_rows(rows, j):
    sub = lax.broadcasted_iota(jnp.int32, (PW, NB), 0)
    cols = [jnp.broadcast_to(rows[:, j + k : j + k + 1], (PW, NB)) for k in range(PW)]
    pivots = jnp.ones((PW, NB), f32)
    left, right = rows[:, :NB], rows[:, NB:]
    for k in range(PW):
        p = jnp.broadcast_to(cols[k][k : k + 1, :], (PW, NB))
        pivots = jnp.where(sub == k, p, pivots)
        if k == PW - 1:
            break
        m = jnp.where(sub > k, cols[k] * (1.0 / p), 0.0)
        left = left - m * left[k : k + 1, :]
        right = right - m * right[k : k + 1, :]
        for q in range(k + 1, PW):
            cols[q] = cols[q] - m * cols[q][k : k + 1, :]
    s = lax.rsqrt(pivots)
    return jnp.concatenate([left * s, right * s], axis=1)


def factor_block(x_ref):
    for j in range(0, NB, PW):
        rows = factor_rows(x_ref[j : j + PW, :], j)
        x_ref[j : j + PW, :] = rows
        if j + PW < NB:
            mh, ml = halves(rows[:, :NB])
            rh, rl = halves(rows)
            lhs = jnp.concatenate([mh, mh, ml], axis=0)
            rhs = jnp.concatenate([rh, rl, rh], axis=0)
            upd = lax.dot_general(
                lhs, rhs, (((0,), (0,)), ((), ())), preferred_element_type=f32
            )
            x_ref[j + PW :, :] = x_ref[j + PW :, :] - upd[j + PW :, :]


def factor_kernel(a_ref, o_ref, s_ref, x_ref):
    n = PANEL
    eye = (
        lax.broadcasted_iota(jnp.int32, (n, n), 0)
        == lax.broadcasted_iota(jnp.int32, (n, n), 1)
    ).astype(f32)
    s_ref[:, :n] = a_ref[...]
    s_ref[:, n:] = eye
    lane = lax.broadcasted_iota(jnp.int32, (NB, n), 1)

    def block(b, carry):
        o = pl.multiple_of(b * NB, NB)
        x_ref[:, :NB] = s_ref[pl.ds(o, NB), pl.ds(o, NB)]
        x_ref[:, NB:] = eye[:NB, :NB]
        factor_block(x_ref)
        w = dot3(x_ref[:, NB:], s_ref[pl.ds(o, NB), :], ((1,), (0,)))
        o_ref[pl.ds(o, NB), :] = w[:, n:]

        @pl.when(b < n // NB - 1)
        def _():
            u = jnp.where(lane >= o + NB, w[:, :n], 0.0)
            s_ref[NB:, NB:] = s_ref[NB:, NB:] - dot3(u[:, NB:], w[:, NB:], ((0,), (0,)))

        return carry

    lax.fori_loop(0, n // NB, block, 0)


def inverse_factor(a):
    return pl.pallas_call(
        factor_kernel,
        out_shape=jax.ShapeDtypeStruct((PANEL, PANEL), f32),
        in_specs=[pl.BlockSpec(memory_space=pltpu.VMEM)],
        out_specs=pl.BlockSpec(memory_space=pltpu.VMEM),
        scratch_shapes=[
            pltpu.VMEM((PANEL, 2 * PANEL), f32),
            pltpu.VMEM((NB, 2 * NB), f32),
        ],
        compiler_params=pltpu.CompilerParams(vmem_limit_bytes=32 << 20),
        name="inverse_factor",
    )(a)


def wire_halves(x):
    hi = lax.reduce_precision(x, 8, 7)
    return hi.astype(bf16), (x - hi).astype(bf16)


def gather(x, axis):
    n = lax.axis_size(axis)
    return lax.all_to_all(jnp.broadcast_to(x[None], (n,) + x.shape), axis, 0, 0, tiled=True)


def gather_ring(x, axis):
    n = lax.axis_size(axis)
    me = lax.axis_index(axis)

    def shift(v, k):
        return lax.ppermute(v, axis, [(i, (i + k) % n) for i in range(n)])

    def put(out, v, k):
        return lax.dynamic_update_index_in_dim(out, v, lax.rem(me + n - k, n), 0)

    parts = {0: x}
    for k in (2, -2, 1, -1):
        parts[k] = shift(x, k)
    parts[3] = shift(parts[2], 1)
    parts[-3] = shift(parts[-2], -1)
    h = x.shape[0] // 2
    parts[4] = jnp.concatenate([shift(parts[2][:h], 2), shift(parts[-2][h:], -2)])
    out = jnp.zeros((n,) + x.shape, x.dtype)
    for k, v in parts.items():
        out = put(out, v, k)
    return out


def gram(a, b):
    return lax.dot_general(a, b, (((0,), (0,)), ((), ())), preferred_element_type=f32)


def per_device(acts, grads, proj_in, proj_out, curvature):
    tp_n, row_n, col_n = (lax.axis_size(a) for a in ("tp", "row", "col"))
    tp = lax.axis_index("tp")
    ex_dev, seq_len, width = acts.shape
    rows_blk, cols_blk = curvature.shape
    act_width, grad_width = proj_in.shape[1], proj_out.shape[1]
    scale = (seq_len * ex_dev * row_n * col_n) ** (-0.5)
    blocks = tp_n * col_n
    piece = PANEL // row_n
    ex = ex_dev // tp_n
    axes = ("tp", "row", "col")
    swap = [(0, 1), (1, 0)]
    first = tp == 0

    def flat(r, b):
        return ((b // col_n) * row_n + r) * col_n + b % col_n

    turn = [(flat(r, b), flat(b, r)) for r in range(row_n) for b in range(blocks)]

    side = int(row_n**0.5)
    lead = curvature[:PANEL].reshape(side, side, piece, cols_blk)
    row = lax.axis_index("row")
    got = [lax.ppermute(lead[k], "row", [(0, side * k)]) for k in range(1, side)]
    lead = jnp.where(row == 0, lead[0], sum(got))
    got = sum(
        lax.ppermute(lead[k], "row", [(side * j, side * j + k) for j in range(side)])
        for k in range(1, side)
    )
    piece_col = jnp.where(lax.rem(row, side) == 0, lead[0], got)

    part = jnp.concatenate(
        [
            jnp.dot(acts.reshape(-1, width), proj_in, preferred_element_type=f32),
            jnp.dot(grads.reshape(-1, width), proj_out, preferred_element_type=f32),
        ],
        axis=1,
    ).reshape(tp_n, ex, seq_len, act_width + grad_width)
    keep = jnp.where(first, part[0], part[1])
    give = jnp.where(first, part[1], part[0])
    proj = keep + lax.ppermute(give, "tp", swap)
    feats = (
        jnp.einsum(
            "esi,esj->eij", proj[..., :act_width], proj[..., act_width:], precision=HIGHEST
        )
        * scale
    ).astype(bf16)
    feats = feats.reshape(ex, act_width * grad_width)

    by_block = feats.reshape(ex, blocks, cols_blk).transpose(1, 0, 2)
    lead_feats = jnp.broadcast_to(feats[None, :, :PANEL], (blocks, ex, PANEL))
    out = jnp.concatenate([by_block, lead_feats], axis=2)
    got = lax.all_to_all(out, ("tp", "col"), 0, 0, tiled=True)
    got = got.reshape(blocks * ex, cols_blk + PANEL)

    n_ex = got.shape[0]
    col_all = gather(got, "row").reshape(row_n * n_ex, -1)
    col_all, lead_piece = lax.optimization_barrier((col_all, piece_col))
    col_feats, lead_feats = col_all[:, :cols_blk], col_all[:, cols_blk:]

    both = jnp.concatenate([got[:, :cols_blk], *wire_halves(piece_col)], axis=0)
    both = lax.ppermute(both, axes, turn)
    diag = both[n_ex:, :PANEL]
    got_diag = sum(
        lax.ppermute(diag, "row", [(0, side * k)]) for k in range(1, side)
    )
    diag = jnp.where(row == 0, diag, got_diag)
    got_diag = sum(
        lax.ppermute(diag, "row", [(side * j, side * j + k) for j in range(side)])
        for k in range(1, side)
    )
    diag = jnp.where(lax.rem(row, side) == 0, diag, got_diag)
    diag = jnp.pad(diag, ((0, 0), (0, rows_blk - PANEL)))
    mine = lax.optimization_barrier(jnp.concatenate([both, diag], axis=0))
    mine = gather_ring(mine, "col")
    lead_col = gather(lead_piece, "row").reshape(-1, cols_blk)

    theirs = lax.ppermute(mine, "tp", swap)
    low, high = jnp.where(first, mine, theirs), jnp.where(first, theirs, mine)
    row_feats, lead_row, diag = [], [], []
    for x in (low, high):
        row_feats.append(x[:, :n_ex].reshape(-1, rows_blk))
        c = x[:, n_ex : n_ex + 2 * piece].astype(f32)
        lead_row.append((c[:, :piece] + c[:, piece:]).reshape(-1, rows_blk))
        d = x[:, n_ex + 2 * piece :, :PANEL].astype(f32)
        diag.append((d[:, :piece] + d[:, piece:]).reshape(-1, PANEL))
    row_feats, lead_row, diag = (jnp.concatenate(v) for v in (row_feats, lead_row, diag))

    inv = inverse_factor(diag + gram(lead_feats, lead_feats))
    panel_row = jnp.dot(inv, lead_row + gram(lead_feats, row_feats), precision=HIGH)
    panel_col = jnp.dot(inv, lead_col + gram(lead_feats, col_feats), precision=HIGH)
    trailing = (
        curvature
        + gram(row_feats, col_feats)
        - lax.dot_general(
            panel_row, panel_col, (((0,), (0,)), ((), ())), precision=HIGH
        )
    )
    half = PANEL // tp_n
    panel = lax.dynamic_slice_in_dim(panel_row, tp * half, half, 0).T
    return (trailing, panel)


def solution(mesh):
    in_specs = (
        P(("row", "col"), None, "tp"),
        P(("row", "col"), None, "tp"),
        P("tp", None),
        P("tp", None),
        P("row", ("tp", "col")),
    )
    out_specs = (P("row", ("tp", "col")), P("row", "tp"))

    return jax.shard_map(
        per_device, mesh=mesh, in_specs=in_specs, out_specs=out_specs, check_vma=False
    )
```

```python
import jax
import jax.numpy as jnp
from jax import lax
from jax.experimental import pallas as pl
from jax.experimental.pallas import tpu as pltpu
from jax.sharding import PartitionSpec as P


PANEL = 512
NB = 128
PW = 16
f32 = jnp.float32
bf16 = jnp.bfloat16
HIGHEST = lax.Precision.HIGHEST
HIGH = lax.Precision.HIGH


def halves(x):
    hi = x.astype(bf16)
    return hi, (x - hi.astype(f32)).astype(bf16)


def dot3(a, b, dims):
    ah, al = halves(a)
    bh, bl = halves(b)

    def d(x, y):
        return lax.dot_general(x, y, (dims, ((), ())), preferred_element_type=f32)

    return d(ah, bh) + (d(ah, bl) + d(al, bh))


def factor_rows(rows, j):
    sub = lax.broadcasted_iota(jnp.int32, (PW, NB), 0)
    cols = [jnp.broadcast_to(rows[:, j + k : j + k + 1], (PW, NB)) for k in range(PW)]
    pivots = jnp.ones((PW, NB), f32)
    left, right = rows[:, :NB], rows[:, NB:]
    for k in range(PW):
        p = jnp.broadcast_to(cols[k][k : k + 1, :], (PW, NB))
        pivots = jnp.where(sub == k, p, pivots)
        if k == PW - 1:
            break
        m = jnp.where(sub > k, cols[k] * (1.0 / p), 0.0)
        left = left - m * left[k : k + 1, :]
        right = right - m * right[k : k + 1, :]
        for q in range(k + 1, PW):
            cols[q] = cols[q] - m * cols[q][k : k + 1, :]
    s = lax.rsqrt(pivots)
    return jnp.concatenate([left * s, right * s], axis=1)


def factor_block(x_ref):
    for j in range(0, NB, PW):
        rows = factor_rows(x_ref[j : j + PW, :], j)
        x_ref[j : j + PW, :] = rows
        if j + PW < NB:
            mh, ml = halves(rows[:, :NB])
            rh, rl = halves(rows)
            lhs = jnp.concatenate([mh, mh, ml], axis=0)
            rhs = jnp.concatenate([rh, rl, rh], axis=0)
            upd = lax.dot_general(
                lhs, rhs, (((0,), (0,)), ((), ())), preferred_element_type=f32
            )
            x_ref[j + PW :, :] = x_ref[j + PW :, :] - upd[j + PW :, :]


def factor_kernel(a_ref, o_ref, s_ref, x_ref):
    n = PANEL
    eye = (
        lax.broadcasted_iota(jnp.int32, (n, n), 0)
        == lax.broadcasted_iota(jnp.int32, (n, n), 1)
    ).astype(f32)
    s_ref[:, :n] = a_ref[...]
    s_ref[:, n:] = eye
    lane = lax.broadcasted_iota(jnp.int32, (NB, n), 1)

    def block(b, carry):
        o = pl.multiple_of(b * NB, NB)
        x_ref[:, :NB] = s_ref[pl.ds(o, NB), pl.ds(o, NB)]
        x_ref[:, NB:] = eye[:NB, :NB]
        factor_block(x_ref)
        w = dot3(x_ref[:, NB:], s_ref[pl.ds(o, NB), :], ((1,), (0,)))
        o_ref[pl.ds(o, NB), :] = w[:, n:]

        @pl.when(b < n // NB - 1)
        def _():
            u = jnp.where(lane >= o + NB, w[:, :n], 0.0)
            s_ref[NB:, NB:] = s_ref[NB:, NB:] - dot3(u[:, NB:], w[:, NB:], ((0,), (0,)))

        return carry

    lax.fori_loop(0, n // NB, block, 0)


def inverse_factor(a):
    return pl.pallas_call(
        factor_kernel,
        out_shape=jax.ShapeDtypeStruct((PANEL, PANEL), f32),
        in_specs=[pl.BlockSpec(memory_space=pltpu.VMEM)],
        out_specs=pl.BlockSpec(memory_space=pltpu.VMEM),
        scratch_shapes=[
            pltpu.VMEM((PANEL, 2 * PANEL), f32),
            pltpu.VMEM((NB, 2 * NB), f32),
        ],
        compiler_params=pltpu.CompilerParams(vmem_limit_bytes=32 << 20),
        name="inverse_factor",
    )(a)


def wire_halves(x):
    hi = lax.reduce_precision(x, 8, 7)
    return hi.astype(bf16), (x - hi).astype(bf16)


def gather(x, axis):
    n = lax.axis_size(axis)
    return lax.all_to_all(jnp.broadcast_to(x[None], (n,) + x.shape), axis, 0, 0, tiled=True)


def gather_ring(x, axis):
    n = lax.axis_size(axis)
    me = lax.axis_index(axis)

    def shift(v, k):
        return lax.ppermute(v, axis, [(i, (i + k) % n) for i in range(n)])

    def put(out, v, k):
        return lax.dynamic_update_index_in_dim(out, v, lax.rem(me + n - k, n), 0)

    parts = {0: x}
    for k in (2, -2, 1, -1):
        parts[k] = shift(x, k)
    parts[3] = shift(parts[2], 1)
    parts[-3] = shift(parts[-2], -1)
    h = x.shape[0] // 2
    parts[4] = jnp.concatenate([shift(parts[2][:h], 2), shift(parts[-2][h:], -2)])
    out = jnp.zeros((n,) + x.shape, x.dtype)
    for k, v in parts.items():
        out = put(out, v, k)
    return out


def gram(a, b):
    return lax.dot_general(a, b, (((0,), (0,)), ((), ())), preferred_element_type=f32)


def per_device(acts, grads, proj_in, proj_out, curvature):
    tp_n, row_n, col_n = (lax.axis_size(a) for a in ("tp", "row", "col"))
    tp = lax.axis_index("tp")
    ex_dev, seq_len, width = acts.shape
    rows_blk, cols_blk = curvature.shape
    act_width, grad_width = proj_in.shape[1], proj_out.shape[1]
    scale = (seq_len * ex_dev * row_n * col_n) ** (-0.5)
    blocks = tp_n * col_n
    piece = PANEL // row_n
    ex = ex_dev // tp_n
    axes = ("tp", "row", "col")
    swap = [(0, 1), (1, 0)]
    first = tp == 0

    def flat(r, b):
        return ((b // col_n) * row_n + r) * col_n + b % col_n

    turn = [(flat(r, b), flat(b, r)) for r in range(row_n) for b in range(blocks)]

    side = int(row_n**0.5)
    lead = curvature[:PANEL].reshape(side, side, piece, cols_blk)
    row = lax.axis_index("row")
    got = [lax.ppermute(lead[k], "row", [(0, side * k)]) for k in range(1, side)]
    lead = jnp.where(row == 0, lead[0], sum(got))
    got = sum(
        lax.ppermute(lead[k], "row", [(side * j, side * j + k) for j in range(side)])
        for k in range(1, side)
    )
    piece_col = jnp.where(lax.rem(row, side) == 0, lead[0], got)

    part = jnp.concatenate(
        [
            jnp.dot(acts.reshape(-1, width), proj_in, preferred_element_type=f32),
            jnp.dot(grads.reshape(-1, width), proj_out, preferred_element_type=f32),
        ],
        axis=1,
    ).reshape(tp_n, ex, seq_len, act_width + grad_width)
    keep = jnp.where(first, part[0], part[1])
    give = jnp.where(first, part[1], part[0])
    proj = keep + lax.ppermute(give, "tp", swap)
    feats = (
        jnp.einsum(
            "esi,esj->eij", proj[..., :act_width], proj[..., act_width:], precision=HIGHEST
        )
        * scale
    ).astype(bf16)
    feats = feats.reshape(ex, act_width * grad_width)

    by_block = feats.reshape(ex, blocks, cols_blk).transpose(1, 0, 2)
    lead_feats = jnp.broadcast_to(feats[None, :, :PANEL], (blocks, ex, PANEL))
    out = jnp.concatenate([by_block, lead_feats], axis=2)
    got = lax.all_to_all(out, ("tp", "col"), 0, 0, tiled=True)
    got = got.reshape(blocks * ex, cols_blk + PANEL)

    n_ex = got.shape[0]
    col_all = gather(got, "row").reshape(row_n * n_ex, -1)
    col_all, lead_piece = lax.optimization_barrier((col_all, piece_col))
    col_feats, lead_feats = col_all[:, :cols_blk], col_all[:, cols_blk:]

    halved = jnp.concatenate(wire_halves(piece_col), axis=0)
    both = jnp.concatenate([got[:, :cols_blk], halved], axis=1)
    both = lax.ppermute(both, axes, turn)
    diag = both[:, cols_blk : cols_blk + PANEL]
    got_diag = sum(
        lax.ppermute(diag, "row", [(0, side * k)]) for k in range(1, side)
    )
    diag = jnp.where(row == 0, diag, got_diag)
    got_diag = sum(
        lax.ppermute(diag, "row", [(side * j, side * j + k) for j in range(side)])
        for k in range(1, side)
    )
    diag = jnp.where(lax.rem(row, side) == 0, diag, got_diag)
    mine = lax.optimization_barrier(jnp.concatenate([both, diag], axis=1))
    mine = gather_ring(mine, "col")
    lead_col = gather(lead_piece, "row").reshape(-1, cols_blk)

    gram_lead = gram(lead_feats, col_all)
    mine, gram_lead = lax.optimization_barrier((mine, gram_lead))
    theirs = lax.ppermute(mine, "tp", swap)
    low, high = jnp.where(first, mine, theirs), jnp.where(first, theirs, mine)
    row_feats, lead_row, diag = [], [], []
    for x in (low, high):
        row_feats.append(x[:, :, :rows_blk].reshape(-1, rows_blk))
        x = x[:, :, rows_blk:].astype(f32)
        x = x[:, :piece] + x[:, piece:]
        lead_row.append(x[:, :, :rows_blk].reshape(-1, rows_blk))
        diag.append(x[:, :, rows_blk:].reshape(-1, PANEL))
    row_feats, lead_row, diag = (jnp.concatenate(v) for v in (row_feats, lead_row, diag))

    inv = inverse_factor(diag + gram_lead[:, cols_blk:])
    inv, lead_col = lax.optimization_barrier((inv, lead_col))
    panel_row = jnp.dot(inv, lead_row + gram(lead_feats, row_feats), precision=HIGH)
    panel_col = jnp.dot(inv, lead_col + gram_lead[:, :cols_blk], precision=HIGH)
    trailing = (
        curvature
        + gram(row_feats, col_feats)
        - lax.dot_general(
            panel_row, panel_col, (((0,), (0,)), ((), ())), precision=HIGH
        )
    )
    half = PANEL // tp_n
    panel = lax.dynamic_slice_in_dim(panel_row, tp * half, half, 0).T
    return (trailing, panel)


def solution(mesh):
    in_specs = (
        P(("row", "col"), None, "tp"),
        P(("row", "col"), None, "tp"),
        P("tp", None),
        P("tp", None),
        P("row", ("tp", "col")),
    )
    out_specs = (P("row", ("tp", "col")), P("row", "tp"))

    return jax.shard_map(
        per_device, mesh=mesh, in_specs=in_specs, out_specs=out_specs, check_vma=False
    )
```

```python
import jax
import jax.numpy as jnp
from jax import lax
from jax.experimental import pallas as pl
from jax.experimental.pallas import tpu as pltpu
from jax.sharding import PartitionSpec as P


PANEL = 512
NB = 128
PW = 16
f32 = jnp.float32
bf16 = jnp.bfloat16
HIGHEST = lax.Precision.HIGHEST
HIGH = lax.Precision.HIGH


def halves(x):
    hi = x.astype(bf16)
    return hi, (x - hi.astype(f32)).astype(bf16)


def dot3(a, b, dims):
    ah, al = halves(a)
    bh, bl = halves(b)

    def d(x, y):
        return lax.dot_general(x, y, (dims, ((), ())), preferred_element_type=f32)

    return d(ah, bh) + (d(ah, bl) + d(al, bh))


def factor_rows(rows, j):
    sub = lax.broadcasted_iota(jnp.int32, (PW, NB), 0)
    cols = [jnp.broadcast_to(rows[:, j + k : j + k + 1], (PW, NB)) for k in range(PW)]
    pivots = jnp.ones((PW, NB), f32)
    left, right = rows[:, :NB], rows[:, NB:]
    for k in range(PW):
        p = jnp.broadcast_to(cols[k][k : k + 1, :], (PW, NB))
        pivots = jnp.where(sub == k, p, pivots)
        if k == PW - 1:
            break
        m = jnp.where(sub > k, cols[k] * (1.0 / p), 0.0)
        left = left - m * left[k : k + 1, :]
        right = right - m * right[k : k + 1, :]
        for q in range(k + 1, PW):
            cols[q] = cols[q] - m * cols[q][k : k + 1, :]
    s = lax.rsqrt(pivots)
    return jnp.concatenate([left * s, right * s], axis=1)


def factor_block(x_ref):
    for j in range(0, NB, PW):
        rows = factor_rows(x_ref[j : j + PW, :], j)
        x_ref[j : j + PW, :] = rows
        if j + PW < NB:
            mh, ml = halves(rows[:, :NB])
            rh, rl = halves(rows)
            lhs = jnp.concatenate([mh, mh, ml], axis=0)
            rhs = jnp.concatenate([rh, rl, rh], axis=0)
            upd = lax.dot_general(
                lhs, rhs, (((0,), (0,)), ((), ())), preferred_element_type=f32
            )
            x_ref[j + PW :, :] = x_ref[j + PW :, :] - upd[j + PW :, :]


def factor_kernel(a_ref, o_ref, s_ref, x_ref):
    n = PANEL
    eye = (
        lax.broadcasted_iota(jnp.int32, (n, n), 0)
        == lax.broadcasted_iota(jnp.int32, (n, n), 1)
    ).astype(f32)
    s_ref[:, :n] = a_ref[...]
    s_ref[:, n:] = eye
    lane = lax.broadcasted_iota(jnp.int32, (NB, n), 1)

    def block(b, carry):
        o = pl.multiple_of(b * NB, NB)
        x_ref[:, :NB] = s_ref[pl.ds(o, NB), pl.ds(o, NB)]
        x_ref[:, NB:] = eye[:NB, :NB]
        factor_block(x_ref)
        w = dot3(x_ref[:, NB:], s_ref[pl.ds(o, NB), :], ((1,), (0,)))
        o_ref[pl.ds(o, NB), :] = w[:, n:]

        @pl.when(b < n // NB - 1)
        def _():
            u = jnp.where(lane >= o + NB, w[:, :n], 0.0)
            s_ref[NB:, NB:] = s_ref[NB:, NB:] - dot3(u[:, NB:], w[:, NB:], ((0,), (0,)))

        return carry

    lax.fori_loop(0, n // NB, block, 0)


def inverse_factor(a):
    return pl.pallas_call(
        factor_kernel,
        out_shape=jax.ShapeDtypeStruct((PANEL, PANEL), f32),
        in_specs=[pl.BlockSpec(memory_space=pltpu.VMEM)],
        out_specs=pl.BlockSpec(memory_space=pltpu.VMEM),
        scratch_shapes=[
            pltpu.VMEM((PANEL, 2 * PANEL), f32),
            pltpu.VMEM((NB, 2 * NB), f32),
        ],
        compiler_params=pltpu.CompilerParams(vmem_limit_bytes=32 << 20),
        name="inverse_factor",
    )(a)


def wire_halves(x):
    hi = lax.reduce_precision(x, 8, 7)
    return hi.astype(bf16), (x - hi).astype(bf16)


def gather(x, axis):
    n = lax.axis_size(axis)
    return lax.all_to_all(jnp.broadcast_to(x[None], (n,) + x.shape), axis, 0, 0, tiled=True)


def gather_ring(x, axis):
    n = lax.axis_size(axis)
    me = lax.axis_index(axis)

    def shift(v, k):
        return lax.ppermute(v, axis, [(i, (i + k) % n) for i in range(n)])

    def put(out, v, k):
        return lax.dynamic_update_index_in_dim(out, v, lax.rem(me + n - k, n), 0)

    parts = {0: x}
    for k in (2, -2, 1, -1):
        parts[k] = shift(x, k)
    parts[3] = shift(parts[2], 1)
    parts[-3] = shift(parts[-2], -1)
    h = x.shape[0] // 2
    parts[4] = jnp.concatenate([shift(parts[2][:h], 2), shift(parts[-2][h:], -2)])
    out = jnp.zeros((n,) + x.shape, x.dtype)
    for k, v in parts.items():
        out = put(out, v, k)
    return out


def gram(a, b):
    return lax.dot_general(a, b, (((0,), (0,)), ((), ())), preferred_element_type=f32)


def per_device(acts, grads, proj_in, proj_out, curvature):
    tp_n, row_n, col_n = (lax.axis_size(a) for a in ("tp", "row", "col"))
    tp = lax.axis_index("tp")
    ex_dev, seq_len, width = acts.shape
    rows_blk, cols_blk = curvature.shape
    act_width, grad_width = proj_in.shape[1], proj_out.shape[1]
    scale = (seq_len * ex_dev * row_n * col_n) ** (-0.5)
    blocks = tp_n * col_n
    piece = PANEL // row_n
    ex = ex_dev // tp_n
    axes = ("tp", "row", "col")
    swap = [(0, 1), (1, 0)]
    first = tp == 0

    def flat(r, b):
        return ((b // col_n) * row_n + r) * col_n + b % col_n

    turn = [(flat(r, b), flat(b, r)) for r in range(row_n) for b in range(blocks)]

    side = int(row_n**0.5)
    lead = curvature[:PANEL].reshape(side, side, piece, cols_blk)
    row = lax.axis_index("row")
    got = [lax.ppermute(lead[k], "row", [(0, side * k)]) for k in range(1, side)]
    lead = jnp.where(row == 0, lead[0], sum(got))
    got = sum(
        lax.ppermute(lead[k], "row", [(side * j, side * j + k) for j in range(side)])
        for k in range(1, side)
    )
    piece_col = jnp.where(lax.rem(row, side) == 0, lead[0], got)

    part = jnp.concatenate(
        [
            jnp.dot(acts.reshape(-1, width), proj_in, preferred_element_type=f32),
            jnp.dot(grads.reshape(-1, width), proj_out, preferred_element_type=f32),
        ],
        axis=1,
    ).reshape(tp_n, ex, seq_len, act_width + grad_width)
    keep = jnp.where(first, part[0], part[1])
    give = jnp.where(first, part[1], part[0])
    proj = keep + lax.ppermute(give, "tp", swap)
    feats = (
        jnp.einsum(
            "esi,esj->eij", proj[..., :act_width], proj[..., act_width:], precision=HIGHEST
        )
        * scale
    ).astype(bf16)
    feats = feats.reshape(ex, act_width * grad_width)

    by_block = feats.reshape(ex, blocks, cols_blk).transpose(1, 0, 2)
    lead_feats = jnp.broadcast_to(feats[None, :, :PANEL], (blocks, ex, PANEL))
    out = jnp.concatenate([by_block, lead_feats], axis=2)
    got = lax.all_to_all(out, ("tp", "col"), 0, 0, tiled=True)
    got = got.reshape(blocks * ex, cols_blk + PANEL)

    n_ex = got.shape[0]
    col_all = gather(got, "row").reshape(row_n * n_ex, -1)
    col_all, lead_piece = lax.optimization_barrier((col_all, piece_col))
    col_feats, lead_feats = col_all[:, :cols_blk], col_all[:, cols_blk:]

    halved = jnp.concatenate(wire_halves(piece_col), axis=0)
    both = jnp.concatenate([got[:, :cols_blk], halved], axis=1)
    both = lax.ppermute(both, axes, turn)
    diag = both[:, cols_blk : cols_blk + PANEL]
    got_diag = sum(
        lax.ppermute(diag, "row", [(0, side * k)]) for k in range(1, side)
    )
    diag = jnp.where(row == 0, diag, got_diag)
    got_diag = sum(
        lax.ppermute(diag, "row", [(side * j, side * j + k) for j in range(side)])
        for k in range(1, side)
    )
    diag = jnp.where(lax.rem(row, side) == 0, diag, got_diag)
    mine = lax.optimization_barrier(jnp.concatenate([both, diag], axis=1))
    mine = gather_ring(mine, "col")
    lead_col = gather(lead_piece, "row").reshape(-1, cols_blk)

    theirs = lax.ppermute(mine, "tp", swap)
    low, high = jnp.where(first, mine, theirs), jnp.where(first, theirs, mine)
    row_feats, lead_row, diag = [], [], []
    for x in (low, high):
        row_feats.append(x[:, :, :rows_blk].reshape(-1, rows_blk))
        x = x[:, :, rows_blk:].astype(f32)
        x = x[:, :piece] + x[:, piece:]
        lead_row.append(x[:, :, :rows_blk].reshape(-1, rows_blk))
        diag.append(x[:, :, rows_blk:].reshape(-1, PANEL))
    row_feats, lead_row, diag = (jnp.concatenate(v) for v in (row_feats, lead_row, diag))

    inv = inverse_factor(diag + gram(lead_feats, lead_feats))
    panel_row = jnp.dot(inv, lead_row + gram(lead_feats, row_feats), precision=HIGH)
    panel_col = jnp.dot(inv, lead_col + gram(lead_feats, col_feats), precision=HIGH)
    trailing = (
        curvature
        + gram(row_feats, col_feats)
        - lax.dot_general(
            panel_row, panel_col, (((0,), (0,)), ((), ())), precision=HIGH
        )
    )
    half = PANEL // tp_n
    panel = lax.dynamic_slice_in_dim(panel_row, tp * half, half, 0).T
    return (trailing, panel)


def solution(mesh):
    in_specs = (
        P(("row", "col"), None, "tp"),
        P(("row", "col"), None, "tp"),
        P("tp", None),
        P("tp", None),
        P("row", ("tp", "col")),
    )
    out_specs = (P("row", ("tp", "col")), P("row", "tp"))

    return jax.shard_map(
        per_device, mesh=mesh, in_specs=in_specs, out_specs=out_specs, check_vma=False
    )
```

```python
import jax
import jax.numpy as jnp
from jax import lax
from jax.experimental import pallas as pl
from jax.experimental.pallas import tpu as pltpu
from jax.sharding import PartitionSpec as P


PANEL = 512
NB = 128
PW = 16
f32 = jnp.float32
bf16 = jnp.bfloat16
HIGHEST = lax.Precision.HIGHEST
HIGH = lax.Precision.HIGH


def halves(x):
    hi = x.astype(bf16)
    return hi, (x - hi.astype(f32)).astype(bf16)


def dot3(a, b, dims):
    ah, al = halves(a)
    bh, bl = halves(b)

    def d(x, y):
        return lax.dot_general(x, y, (dims, ((), ())), preferred_element_type=f32)

    return d(ah, bh) + (d(ah, bl) + d(al, bh))


def factor_rows(rows, j):
    sub = lax.broadcasted_iota(jnp.int32, (PW, NB), 0)
    cols = [jnp.broadcast_to(rows[:, j + k : j + k + 1], (PW, NB)) for k in range(PW)]
    pivots = jnp.ones((PW, NB), f32)
    left, right = rows[:, :NB], rows[:, NB:]
    for k in range(PW):
        p = jnp.broadcast_to(cols[k][k : k + 1, :], (PW, NB))
        pivots = jnp.where(sub == k, p, pivots)
        if k == PW - 1:
            break
        m = jnp.where(sub > k, cols[k] * (1.0 / p), 0.0)
        left = left - m * left[k : k + 1, :]
        right = right - m * right[k : k + 1, :]
        for q in range(k + 1, PW):
            cols[q] = cols[q] - m * cols[q][k : k + 1, :]
    s = lax.rsqrt(pivots)
    return jnp.concatenate([left * s, right * s], axis=1)


def factor_block(x_ref):
    for j in range(0, NB, PW):
        rows = factor_rows(x_ref[j : j + PW, :], j)
        x_ref[j : j + PW, :] = rows
        if j + PW < NB:
            mh, ml = halves(rows[:, :NB])
            rh, rl = halves(rows)
            lhs = jnp.concatenate([mh, mh, ml], axis=0)
            rhs = jnp.concatenate([rh, rl, rh], axis=0)
            upd = lax.dot_general(
                lhs, rhs, (((0,), (0,)), ((), ())), preferred_element_type=f32
            )
            x_ref[j + PW :, :] = x_ref[j + PW :, :] - upd[j + PW :, :]


def factor_kernel(a_ref, o_ref, s_ref, x_ref):
    n = PANEL
    eye = (
        lax.broadcasted_iota(jnp.int32, (n, n), 0)
        == lax.broadcasted_iota(jnp.int32, (n, n), 1)
    ).astype(f32)
    s_ref[:, :n] = a_ref[...]
    s_ref[:, n:] = eye
    lane = lax.broadcasted_iota(jnp.int32, (NB, n), 1)

    def block(b, carry):
        o = pl.multiple_of(b * NB, NB)
        x_ref[:, :NB] = s_ref[pl.ds(o, NB), pl.ds(o, NB)]
        x_ref[:, NB:] = eye[:NB, :NB]
        factor_block(x_ref)
        w = dot3(x_ref[:, NB:], s_ref[pl.ds(o, NB), :], ((1,), (0,)))
        o_ref[pl.ds(o, NB), :] = w[:, n:]

        @pl.when(b < n // NB - 1)
        def _():
            u = jnp.where(lane >= o + NB, w[:, :n], 0.0)
            s_ref[NB:, NB:] = s_ref[NB:, NB:] - dot3(u[:, NB:], w[:, NB:], ((0,), (0,)))

        return carry

    lax.fori_loop(0, n // NB, block, 0)


def inverse_factor(a):
    return pl.pallas_call(
        factor_kernel,
        out_shape=jax.ShapeDtypeStruct((PANEL, PANEL), f32),
        in_specs=[pl.BlockSpec(memory_space=pltpu.VMEM)],
        out_specs=pl.BlockSpec(memory_space=pltpu.VMEM),
        scratch_shapes=[
            pltpu.VMEM((PANEL, 2 * PANEL), f32),
            pltpu.VMEM((NB, 2 * NB), f32),
        ],
        compiler_params=pltpu.CompilerParams(vmem_limit_bytes=32 << 20),
        name="inverse_factor",
    )(a)


def wire_halves(x):
    hi = lax.reduce_precision(x, 8, 7)
    return hi.astype(bf16), (x - hi).astype(bf16)


def gather(x, axis):
    n = lax.axis_size(axis)
    return lax.all_to_all(jnp.broadcast_to(x[None], (n,) + x.shape), axis, 0, 0, tiled=True)


def gather_ring(x, axis):
    n = lax.axis_size(axis)
    me = lax.axis_index(axis)

    def shift(v, k):
        return lax.ppermute(v, axis, [(i, (i + k) % n) for i in range(n)])

    def put(out, v, k):
        return lax.dynamic_update_index_in_dim(out, v, lax.rem(me + n - k, n), 0)

    parts = {0: x}
    for k in (2, -2, 1, -1):
        parts[k] = shift(x, k)
    parts[3] = shift(parts[2], 1)
    parts[-3] = shift(parts[-2], -1)
    h = x.shape[0] // 2
    parts[4] = jnp.concatenate([shift(parts[2][:h], 2), shift(parts[-2][h:], -2)])
    out = jnp.zeros((n,) + x.shape, x.dtype)
    for k, v in parts.items():
        out = put(out, v, k)
    return out


def gram(a, b):
    return lax.dot_general(a, b, (((0,), (0,)), ((), ())), preferred_element_type=f32)


def per_device(acts, grads, proj_in, proj_out, curvature):
    tp_n, row_n, col_n = (lax.axis_size(a) for a in ("tp", "row", "col"))
    tp = lax.axis_index("tp")
    ex_dev, seq_len, width = acts.shape
    rows_blk, cols_blk = curvature.shape
    act_width, grad_width = proj_in.shape[1], proj_out.shape[1]
    scale = (seq_len * ex_dev * row_n * col_n) ** (-0.5)
    blocks = tp_n * col_n
    piece = PANEL // row_n
    ex = ex_dev // tp_n
    axes = ("tp", "row", "col")
    swap = [(0, 1), (1, 0)]
    first = tp == 0

    def flat(r, b):
        return ((b // col_n) * row_n + r) * col_n + b % col_n

    turn = [(flat(r, b), flat(b, r)) for r in range(row_n) for b in range(blocks)]

    side = int(row_n**0.5)
    lead = curvature[:PANEL].reshape(side, side, piece, cols_blk)
    row = lax.axis_index("row")
    got = [lax.ppermute(lead[k], "row", [(0, side * k)]) for k in range(1, side)]
    lead = jnp.where(row == 0, lead[0], sum(got))
    got = sum(
        lax.ppermute(lead[k], "row", [(side * j, side * j + k) for j in range(side)])
        for k in range(1, side)
    )
    piece_col = jnp.where(lax.rem(row, side) == 0, lead[0], got)

    part = jnp.concatenate(
        [
            jnp.dot(acts.reshape(-1, width), proj_in, preferred_element_type=f32),
            jnp.dot(grads.reshape(-1, width), proj_out, preferred_element_type=f32),
        ],
        axis=1,
    ).reshape(tp_n, ex, seq_len, act_width + grad_width)
    keep = jnp.where(first, part[0], part[1])
    give = jnp.where(first, part[1], part[0])
    proj = keep + lax.ppermute(give, "tp", swap)
    feats = (
        jnp.einsum(
            "esi,esj->eij", proj[..., :act_width], proj[..., act_width:], precision=HIGHEST
        )
        * scale
    ).astype(bf16)
    feats = feats.reshape(ex, act_width * grad_width)

    by_block = feats.reshape(ex, blocks, cols_blk).transpose(1, 0, 2)
    lead_feats = jnp.broadcast_to(feats[None, :, :PANEL], (blocks, ex, PANEL))
    out = jnp.concatenate([by_block, lead_feats], axis=2)
    got = lax.all_to_all(out, ("tp", "col"), 0, 0, tiled=True)
    got = got.reshape(blocks * ex, cols_blk + PANEL)

    n_ex = got.shape[0]
    col_all = gather(got, "row").reshape(row_n * n_ex, -1)
    col_all, lead_piece = lax.optimization_barrier((col_all, piece_col))
    col_feats, lead_feats = col_all[:, :cols_blk], col_all[:, cols_blk:]

    piece_row = lax.ppermute(piece_col, axes, turn)
    diag = piece_row[:, :PANEL]
    got_diag = sum(
        lax.ppermute(diag, "row", [(0, side * k)]) for k in range(1, side)
    )
    diag = jnp.where(row == 0, diag, got_diag)
    got_diag = sum(
        lax.ppermute(diag, "row", [(side * j, side * j + k) for j in range(side)])
        for k in range(1, side)
    )
    diag = jnp.where(lax.rem(row, side) == 0, diag, got_diag)
    turned = lax.ppermute(got[:, :cols_blk], axes, turn)
    mine = [turned] + [jnp.concatenate(wire_halves(v), axis=0) for v in (piece_row, diag)]
    mine = lax.optimization_barrier(jnp.concatenate(mine, axis=1))
    mine = gather_ring(mine, "col")
    lead_col = gather(lead_piece, "row").reshape(-1, cols_blk)

    theirs = lax.ppermute(mine, "tp", swap)
    low, high = jnp.where(first, mine, theirs), jnp.where(first, theirs, mine)
    row_feats, lead_row, diag = [], [], []
    for x in (low, high):
        row_feats.append(x[:, :, :rows_blk].reshape(-1, rows_blk))
        x = x[:, :, rows_blk:].astype(f32)
        x = x[:, :piece] + x[:, piece:]
        lead_row.append(x[:, :, :rows_blk].reshape(-1, rows_blk))
        diag.append(x[:, :, rows_blk:].reshape(-1, PANEL))
    row_feats, lead_row, diag = (jnp.concatenate(v) for v in (row_feats, lead_row, diag))

    inv = inverse_factor(diag + gram(lead_feats, lead_feats))
    panel_row = jnp.dot(inv, lead_row + gram(lead_feats, row_feats), precision=HIGH)
    panel_col = jnp.dot(inv, lead_col + gram(lead_feats, col_feats), precision=HIGH)
    trailing = (
        curvature
        + gram(row_feats, col_feats)
        - lax.dot_general(
            panel_row, panel_col, (((0,), (0,)), ((), ())), precision=HIGH
        )
    )
    half = PANEL // tp_n
    panel = lax.dynamic_slice_in_dim(panel_row, tp * half, half, 0).T
    return (trailing, panel)


def solution(mesh):
    in_specs = (
        P(("row", "col"), None, "tp"),
        P(("row", "col"), None, "tp"),
        P("tp", None),
        P("tp", None),
        P("row", ("tp", "col")),
    )
    out_specs = (P("row", ("tp", "col")), P("row", "tp"))

    return jax.shard_map(
        per_device, mesh=mesh, in_specs=in_specs, out_specs=out_specs, check_vma=False
    )
```
